512 devices in a mesh: lon: 32 (over z_lo, x), ch: 16 (over z_hi, y, core).
Axes of the slice: x: 4, y: 4, z: 16 (z_hi: 2, z_lo: 8; z = z_hi * 8 + z_lo), core: 2. Of those that a mesh axis runs over, the one named last changes fastest.
Arguments:
- inputs: bfloat16 [1, 4, 48, 64, 512], P(None, None, None, 'lon', 'ch'), may hold values from -6 to 6
- grad_out: bfloat16 [1, 4, 48, 64, 512], P(None, None, None, 'lon', 'ch'), may hold values from -6 to 6
- kernel: bfloat16 [3, 3, 3, 512, 512], P(None, None, None, 'ch'), may hold values from -0.0546875 to 0.0546875
Outputs:
- grad_in: bfloat16 [1, 4, 48, 64, 512], P(None, None, None, 'lon', 'ch')
- grad_kernel: float32 [3, 3, 3, 512, 512], P(None, None, None, 'ch', 'lon')
The draws below stay inside these ranges and needn't reach their ends.
All inputs are finite; a program needn't handle non-finite values.
Results may differ from the reference program's by a relative error of at most 0.0012.
Values may be sent and summed in bfloat16 or wider, within the bound.
A program may use at most 64 MiB of HBM per device.

```python
import math
import jax
import jax.numpy as jnp

CH = 512
BATCH = 1
FRAMES = 4
LAT = 48
LON = 64


def with_spikes(array, stream_key, source, target, shards_of, factor):
    owner, partner = [(jnp.arange(array.shape[axis_at]) // (array.shape[axis_at] // shards_of)).reshape([-1 if axis == axis_at else 1 for axis in range(array.ndim)]) for axis_at in (source, target)]
    chosen = jax.random.permutation(stream_key, shards_of)[partner]
    strong = (owner == chosen) | (owner == (partner + shards_of // 2) % shards_of)
    return jnp.where(strong, factor * array, array)


def shard_levels(rng, dims, split, smallest, top_value):
    gain, own = 1.0, jax.random.fold_in(rng, 6)
    for dim, blocks in split:
        steps = jnp.exp(jax.random.uniform(jax.random.fold_in(own, dim), (blocks,), jnp.float32, smallest / len(split), top_value / len(split)))
        gain = gain * jnp.repeat(steps, dims[dim] // blocks).reshape([-1 if axis == dim else 1 for axis in range(len(dims))])
    return gain


def scatter_about(rng, extent, width, bound, pieces=(), dtype=jnp.bfloat16):
    loudness = shard_levels(rng, extent, pieces, -0.22, 0.18) if pieces else 1.0
    values = jax.random.normal(rng, extent, jnp.float32) * width * loudness
    return jnp.minimum(jnp.maximum(values, -bound), bound).astype(dtype)


def gaussian_with(stream_key, extent, spread, limit, pieces, heavy, held_as=jnp.bfloat16):
    entries = spread * jax.random.normal(stream_key, extent, jnp.float32)
    if pieces:
        entries = entries * shard_levels(stream_key, extent, pieces, -0.22, 0.18)
    return jnp.clip(with_spikes(entries, jax.random.fold_in(stream_key, 3), *heavy), -limit, limit).astype(held_as)


def setup_inputs(seed: int = 0) -> dict:
    splits = jax.random.split(jax.random.key(seed), 4)
    return {
        "inputs": scatter_about(splits[0], (BATCH, FRAMES, LAT, LON, CH), 1.0, 6.0, ((3, 32), (4, 16))),
        "grad_out": gaussian_with(splits[1], (BATCH, FRAMES, LAT, LON, CH), 1.0, 6.0, ((3, 32), (4, 16)), (3, 4, 32, 2.75)),
        "kernel": scatter_about(splits[2], (3, 3, 3, CH, CH), (27 * CH) ** -0.5, 0.0546875, ((3, 16),)),
    }


def pad_rim(values):
    padded = jnp.pad(values, ((0, 0), (1, 1), (1, 1), (0, 0), (0, 0)))
    return jnp.concatenate([padded[:, :, :, -1:], padded, padded[:, :, :, :1]], axis=3)

def reference(inputs, grad_out, kernel):
    batches, frames, lat_cells, lon_cells, channels = inputs.shape
    input_pad = pad_rim(inputs)
    grad_pad = pad_rim(grad_out)
    flat_grad = grad_out.reshape(-1, channels)
    accum_dx = jnp.zeros((batches * frames * lat_cells * lon_cells, channels), jnp.float32)
    tap_terms = []
    for step_t in range(3):
        for step_h in range(3):
            for step_w in range(3):
                grad_slice = grad_pad[:, 2 - step_t:2 - step_t + frames, 2 - step_h:2 - step_h + lat_cells, 2 - step_w:2 - step_w + lon_cells].reshape(-1, channels)
                accum_dx = accum_dx + jnp.dot(grad_slice, kernel[step_t, step_h, step_w].T, preferred_element_type=jnp.float32)
                x_slice = input_pad[:, step_t:step_t + frames, step_h:step_h + lat_cells, step_w:step_w + lon_cells].reshape(-1, channels)
                tap_terms.append(jnp.dot(x_slice.T, flat_grad, preferred_element_type=jnp.float32))
    grad_in = accum_dx.astype(jnp.bfloat16).reshape(inputs.shape)
    rscale = 1.0 / math.sqrt(batches * frames * lat_cells * lon_cells)
    grad_kernel = jnp.stack(tap_terms).reshape(3, 3, 3, channels, channels) * rscale
    return (grad_in, grad_kernel)
```

```python
import functools
import math

import jax
import jax.numpy as jnp
from jax import lax
from jax.experimental import pallas as pl
from jax.experimental.pallas import tpu as pltpu
from jax.sharding import PartitionSpec as P

NX, NZ, NY, NH = 4, 8, 4, 2
MESH = pl.DeviceIdType.MESH
T, H, W, CI, CO = 4, 48, 2, 32, 16
COL = T * H
POS = W * COL


def shift_lanes(v, s):
    n = v.shape[1]
    s = s % n
    if s == 0:
        return v
    return jnp.concatenate([v[:, n - s:], v[:, :n - s]], axis=1)


def pack(ref):
    return jnp.concatenate([ref[t, w] for w in range(W) for t in range(T)], axis=1)


def kernel(rscale, x_ref, g_ref, k_ref, gin_ref, gk_ref,
           xg, gall, sx, gg, prod, zbuf, zl, zr, acc,
           swap_s, swap_r, gy_s, gy_r, core_s, core_r,
           xz_s, xz_r, xx_s, xx_r, ax_s, ax_r, az_s, az_r, ay_s, ay_r, ac_s, ac_r, ha_s, ha_r):
    lon, ch = lax.axis_index("lon"), lax.axis_index("ch")
    z, x = lon // NX, lon % NX
    zh, y, core = ch // (2 * NY), (ch // 2) % NY, ch % 2

    def at(z=z, x=x, zh=zh, y=y, core=core):
        return (z * NX + x, (zh * NY + y) * 2 + core)

    swap_id = at(zh=1 - zh)
    sib_id = at(core=1 - core)
    left_id = (lax.rem(lon + NX * NZ - 1, NX * NZ), ch)
    right_id = (lax.rem(lon + 1, NX * NZ), ch)
    y_ids = [at(y=lax.rem(y + d, NY)) for d in range(1, NY)]
    z_ids = [at(z=lax.rem(z + d, NZ)) for d in range(1, NZ)]
    x_ids = [at(x=lax.rem(x + d, NX)) for d in range(1, NX)]
    partners = [swap_id, sib_id, left_id, right_id] + y_ids + z_ids + x_ids

    barrier = pltpu.get_barrier_semaphore()
    for dev in partners:
        pl.semaphore_signal(barrier, inc=1, device_id=dev, device_id_type=MESH)

    def remote(src, dst, ss, rs, dev):
        return pltpu.make_async_remote_copy(
            src_ref=src, dst_ref=dst, send_sem=ss, recv_sem=rs, device_id=dev, device_id_type=MESH)

    gall[zh, y, core] = pack(g_ref)
    xg[x, z] = pack(x_ref)
    pl.semaphore_wait(barrier, len(partners))

    sends = []

    def go(copy):
        copy.start()
        sends.append(copy)
        return copy

    mine = gall.at[zh, y, core]
    swap = go(remote(mine, mine, swap_s, swap_r, swap_id))
    gy = [go(remote(mine, mine, gy_s.at[0, d], gy_r.at[0, d], y_ids[d])) for d in range(NY - 1)]
    own = xg.at[x, z]
    xz = [go(remote(own, own, xz_s.at[d], xz_r.at[d], z_ids[d])) for d in range(NZ - 1)]
    xx = []
    for d in range(NX - 1):
        xx.append(go(remote(own, own, xx_s.at[0, d], xx_r.at[0, d], x_ids[d])))
    swap.wait_recv()
    other = gall.at[1 - zh, y, core]
    gy += [go(remote(other, other, gy_s.at[1, d], gy_r.at[1, d], y_ids[d])) for d in range(NY - 1)]
    for c in gy:
        c.wait_recv()
    half = gall.at[:, :, core]
    sib = go(remote(half, half, core_s, core_r, sib_id))

    carries = core == x // 2

    def ax_copy(r, dev):
        return remote(gall.at[:, :, core, pl.ds(CO * r, CO)], sx, ax_s.at[r], ax_r, dev)

    @pl.when(x == y)
    def _():
        for r in range(2):
            xd = core * 2 + r

            @pl.when(xd != x)
            def _():
                ax_copy(r, at(x=xd)).start()

            @pl.when(xd == x)
            def _():
                sx[...] = gall[:, :, core, CO * r:CO * (r + 1)]

    for d in range(NZ - 1):
        xz[d].wait_recv()
        blk = xg.at[x, lax.rem(z + NZ - 1 - d, NZ)]
        for e in range(NX - 1):
            xx.append(go(remote(blk, blk, xx_s.at[d + 1, e], xx_r.at[d + 1, e], x_ids[e])))

    def az_copy(d):
        zd = lax.rem(z + d + 1, NZ)
        return remote(sx.at[zd // NY, lax.rem(zd, NY)], gg.at[y, z], az_s.at[d], az_r.at[d], z_ids[d])

    @pl.when(carries)
    def _():
        @pl.when(x != y)
        def _():
            ax_copy(0, sib_id).wait_recv()
        for d in range(NZ - 1):
            az_copy(d).start()
        gg[y, z] = sx[z // NY, lax.rem(z, NY)]

    sib.wait_recv()
    lane = lax.broadcasted_iota(jnp.int32, (1, POS), 1)
    hh = lax.rem(lane, H)
    tt = lax.rem(lane // H, T)
    low = lane < COL
    prod[...] = jnp.dot(k_ref[...], gall[...].reshape(NH * NY * 2 * CI, POS), preferred_element_type=jnp.float32)

    def tap(a, c, e):
        r = ((a * 3 + c) * 3 + e) * CI
        return prod[r:r + CI, :]

    sums = []
    for e in range(3):
        total = None
        for a in range(3):
            part = tap(a, 1, e)
            part += jnp.where(hh != H - 1, shift_lanes(tap(a, 0, e), -1), 0.0)
            part += jnp.where(hh != 0, shift_lanes(tap(a, 2, e), 1), 0.0)
            if a == 0:
                part = jnp.where(tt != T - 1, shift_lanes(part, -H), 0.0)
            elif a == 2:
                part = jnp.where(tt != 0, shift_lanes(part, H), 0.0)
            total = part if total is None else total + part
        sums.append(total)
    zbuf[...] = jnp.where(low, sums[0], sums[2])
    to_left = go(remote(zbuf, zr, ha_s.at[0], ha_r.at[0], left_id))
    to_right = go(remote(zbuf, zl, ha_s.at[1], ha_r.at[1], right_id))

    def ay_copy(d):
        slab = gg.at[y]
        return remote(slab, slab, ay_s.at[d], ay_r.at[d], y_ids[d])

    def ac_copy(d):
        slab = gg.at[lax.rem(y + NY - d, NY)]
        return remote(slab, slab, ac_s.at[d], ac_r.at[d], sib_id)

    @pl.when(carries)
    def _():
        for d in range(NZ - 1):
            az_copy(d).wait_recv()
        for d in range(NY - 1):
            ay_copy(d).start()
        ac_copy(0).start()
        for d in range(NY - 1):
            ay_copy(d).wait_recv()
            ac_copy(d + 1).start()

    @pl.when(jnp.logical_not(carries))
    def _():
        for d in range(NY):
            ac_copy(d).wait_recv()

    to_left.wait_recv()
    to_right.wait_recv()
    grad = sums[1] + shift_lanes(jnp.where(low, sums[2] + zr[...], sums[0] + zl[...]), COL)
    grad = grad.astype(jnp.bfloat16)
    for w in range(W):
        for t in range(T):
            o = w * COL + t * H
            gin_ref[t, w] = grad[:, o:o + H]

    for c in xx:
        c.wait_recv()

    zero = jnp.zeros((), jnp.bfloat16)
    acc[...] = jnp.zeros_like(acc)

    @pl.loop(0, NZ)
    def _(zz):
        for xs in range(NX):
            xb = xg[xs, zz]
            x0 = jnp.where(hh != 0, shift_lanes(xb, 1), zero)
            x2 = jnp.where(hh != H - 1, shift_lanes(xb, -1), zero)
            rows = jnp.concatenate([x0, xb, x2], axis=0)
            here = gg[xs, zz]
            after = gg[xs + 1, zz] if xs < NX - 1 else gg[0, lax.rem(zz + 1, NZ)]
            before = gg[xs - 1, zz] if xs > 0 else gg[NX - 1, lax.rem(zz + NZ - 1, NZ)]
            rh = shift_lanes(here, COL)
            e0 = jnp.where(low, rh, shift_lanes(after, COL))
            e2 = jnp.where(low, shift_lanes(before, COL), rh)
            ge = jnp.concatenate([e0, here, e2], axis=0)
            a0 = jnp.where(tt != T - 1, shift_lanes(ge, -H), zero)
            a2 = jnp.where(tt != 0, shift_lanes(ge, H), zero)
            gs = jnp.concatenate([a0, ge, a2], axis=0)
            acc[...] += lax.dot_general(gs, rows, (((1,), (1,)), ((), ())), preferred_element_type=jnp.float32)

    for a in range(3):
        for e in range(3):
            r = (a * 3 + e) * CO
            for c in range(3):
                gk_ref[(a * 3 + c) * 3 + e] = acc[r:r + CO, c * CI:(c + 1) * CI] * rscale

    for c in sends:
        c.wait_send()

    @pl.when(x == y)
    def _():
        for r in range(2):
            @pl.when(core * 2 + r != x)
            def _():
                ax_copy(r, sib_id).wait_send()

    @pl.when(carries)
    def _():
        for d in range(NZ - 1):
            az_copy(d).wait_send()
        for d in range(NY - 1):
            ay_copy(d).wait_send()
        for d in range(NY):
            ac_copy(d).wait_send()


def body(inputs, grad_out, weights):
    rscale = 1.0 / math.sqrt(T * H * W * NX * NZ)
    xs = inputs.transpose(0, 1, 3, 4, 2).reshape(T, W, CI, H)
    gs = grad_out.transpose(0, 1, 3, 4, 2).reshape(T, W, CI, H)
    ks = weights.reshape(27 * CI, 512)
    dma = pltpu.SemaphoreType.DMA
    gin, gk = pl.pallas_call(
        functools.partial(kernel, rscale),
        out_shape=(jax.ShapeDtypeStruct((T, W, CI, H), jnp.bfloat16),
                   jax.ShapeDtypeStruct((27, CO, CI), jnp.float32)),
        in_specs=[pl.BlockSpec(memory_space=pltpu.VMEM)] * 3,
        out_specs=(pl.BlockSpec(memory_space=pltpu.VMEM),) * 2,
        scratch_shapes=[
            pltpu.VMEM((NX, NZ, CI, POS), jnp.bfloat16),
            pltpu.VMEM((NH, NY, 2, CI, POS), jnp.bfloat16),
            pltpu.VMEM((NH, NY, CO, POS), jnp.bfloat16),
            pltpu.VMEM((NX, NZ, CO, POS), jnp.bfloat16),
            pltpu.VMEM((27 * CI, POS), jnp.float32),
            pltpu.VMEM((CI, POS), jnp.float32),
            pltpu.VMEM((CI, POS), jnp.float32),
            pltpu.VMEM((CI, POS), jnp.float32),
            pltpu.VMEM((9 * CO, 3 * CI), jnp.float32),
            dma, dma, dma((2, NY - 1)), dma((2, NY - 1)), dma, dma,
            dma((NZ - 1,)), dma((NZ - 1,)), dma((NZ, NX - 1)), dma((NZ, NX - 1)),
            dma((2,)), dma, dma((NZ - 1,)), dma((NZ - 1,)),
            dma((NY - 1,)), dma((NY - 1,)), dma((NY,)), dma((NY,)), dma((2,)), dma((2,)),
        ],
        compiler_params=pltpu.CompilerParams(
            collective_id=0, has_side_effects=True, vmem_limit_bytes=32 << 20),
    )(xs, gs, ks)
    grad_in = gin.reshape(1, T, W, CI, H).transpose(0, 1, 4, 2, 3)
    grad_kernel = gk.reshape(3, 3, 3, CO, CI).transpose(0, 1, 2, 4, 3)
    return grad_in, grad_kernel


def solution(mesh):
    return jax.shard_map(
        body,
        mesh=mesh,
        in_specs=(
            P(None, None, None, "lon", "ch"),
            P(None, None, None, "lon", "ch"),
            P(None, None, None, "ch", None),
        ),
        out_specs=(P(None, None, None, "lon", "ch"), P(None, None, None, "ch", "lon")),
        check_vma=False,
    )
```

```python
import functools
import math

import jax
import jax.numpy as jnp
from jax import lax
from jax.experimental import pallas as pl
from jax.experimental.pallas import tpu as pltpu
from jax.sharding import PartitionSpec as P

NX, NZ, NY, NH = 4, 8, 4, 2
MESH = pl.DeviceIdType.MESH
T, H, W, CI, CO = 4, 48, 2, 32, 16
COL = T * H
POS = W * COL
HALF = NY * 2 * CI
NEAR = (0, 6, 1, 5, 2, 4, 3)


def shift_lanes(v, s):
    n = v.shape[1]
    s = s % n
    if s == 0:
        return v
    return jnp.concatenate([v[:, n - s:], v[:, :n - s]], axis=1)


def pack(ref):
    return jnp.concatenate([ref[t, w] for w in range(W) for t in range(T)], axis=1)


def kernel(rscale, x_hbm, g_hbm, k_hbm, gin_ref, gk_ref,
           x_ref, g_ref, k_ref, xg, xs, gall, abuf, gg, prod, zbuf, zl, zr, acc,
           load_s, swap_s, swap_r, gy_s, gy_r, core_s, core_r,
           xz_s, xz_r, xx_s, xx_r, a_s, a_r, b_s, b_r, ay_s, ay_r, ac_s, ac_r, ha_s, ha_r):
    lon, ch = lax.axis_index("lon"), lax.axis_index("ch")
    z, x = lon // NX, lax.rem(lon, NX)
    zh, y, core = ch // (2 * NY), lax.rem(ch // 2, NY), lax.rem(ch, 2)

    def at(z=z, x=x, zh=zh, y=y, core=core):
        return (z * NX + x, (zh * NY + y) * 2 + core)

    swap_id = at(zh=1 - zh)
    sib_id = at(core=1 - core)
    left_id = (lax.rem(lon + NX * NZ - 1, NX * NZ), ch)
    right_id = (lax.rem(lon + 1, NX * NZ), ch)
    y_ids = [at(y=lax.rem(y + d, NY)) for d in range(1, NY)]
    z_ids = [at(z=lax.rem(z + d, NZ)) for d in range(1, NZ)]
    x_ids = [at(x=lax.rem(x + d, NX)) for d in range(1, NX)]
    partners = [swap_id, sib_id, left_id, right_id] + y_ids + z_ids + x_ids

    turn = y == lax.rem(z, NY)
    home = zh == z // NY
    carries = core == x // 2
    b_from = at(x=y, y=lax.rem(z, NY))
    b_self = turn & (x == y)

    barrier = pltpu.get_barrier_semaphore()

    def greet(dev):
        pl.semaphore_signal(barrier, inc=1, device_id=dev, device_id_type=MESH)

    for dev in partners:
        greet(dev)

    @pl.when(turn & jnp.logical_not(home))
    def _():
        for s in range(NZ):
            greet(at(z=s, zh=1 - zh))

    @pl.when(carries & jnp.logical_not(b_self))
    def _():
        greet(b_from)

    load_g = pltpu.make_async_copy(g_hbm, g_ref, load_s.at[0])
    load_x = pltpu.make_async_copy(x_hbm, x_ref, load_s.at[1])
    load_k = pltpu.make_async_copy(k_hbm, k_ref, load_s.at[2])
    load_g.start()
    load_x.start()
    load_k.start()

    def remote(src, dst, ss, rs, dev):
        return pltpu.make_async_remote_copy(
            src_ref=src, dst_ref=dst, send_sem=ss, recv_sem=rs, device_id=dev, device_id_type=MESH)

    load_g.wait()
    gall[zh, y, core] = pack(g_ref)
    load_x.wait()
    xg[x, z] = pack(x_ref)
    pl.semaphore_wait(barrier, len(partners) + 1 + jnp.where(turn, 2 - (carries & (x == y)).astype(jnp.int32), 0))

    sends = []

    def go(copy):
        copy.start()
        sends.append(copy)
        return copy

    mine = gall.at[zh, y, core]
    swap = go(remote(mine, mine, swap_s, swap_r, swap_id))
    a_z = zh * NY + y
    go(remote(mine, abuf.at[z], a_s.at[0], a_r.at[z], at(z=a_z, zh=1 - zh)))

    def a_near():
        return remote(mine, abuf.at[z], a_s.at[1], a_r.at[z], at(z=a_z))

    @pl.when(a_z != z)
    def _():
        a_near().start()

    @pl.when(a_z == z)
    def _():
        abuf[z] = gall[zh, y, core]

    gy = [go(remote(mine, mine, gy_s.at[0, d], gy_r.at[0, d], y_ids[d])) for d in range(NY - 1)]
    own = xg.at[x, z]
    xz = {d: go(remote(own, own, xz_s.at[d], xz_r.at[d], z_ids[d])) for d in NEAR}
    xx = [go(remote(own, own, xx_s.at[0, e], xx_r.at[0, e], x_ids[e])) for e in range(NX - 1)]

    def pass_x(ds):
        for d in ds:
            xz[d].wait_recv()
            blk = xg.at[x, lax.rem(z + NZ - 1 - d, NZ)]
            for e in range(NX - 1):
                xx.append(go(remote(blk, blk, xx_s.at[d + 1, e], xx_r.at[d + 1, e], x_ids[e])))

    def to_core(h, i):
        part = gall.at[h, :, core]
        return go(remote(part, part, core_s.at[i], core_r.at[i], sib_id))

    for c in gy:
        c.wait_recv()
    sib0 = to_core(zh, 0)
    pass_x(NEAR[:4])

    swap.wait_recv()
    other = gall.at[1 - zh, y, core]
    gy1 = [go(remote(other, other, gy_s.at[1, d], gy_r.at[1, d], y_ids[d])) for d in range(NY - 1)]

    def b_copy(r):
        return remote(abuf.at[:, pl.ds(CO * r, CO)], gg.at[x], b_s.at[r], b_r, at(x=core * 2 + r, y=x))

    def b_here(r):
        return (core * 2 + r == x) & (x == y)

    @pl.when(turn)
    def _():
        for s in range(NZ):
            @pl.when(jnp.logical_not(home & (z == s)))
            def _():
                remote(mine, abuf.at[s], a_s.at[0], a_r.at[s], sib_id).wait_recv()
        for r in range(2):
            @pl.when(jnp.logical_not(b_here(r)))
            def _():
                b_copy(r).start()

            @pl.when(b_here(r))
            def _():
                gg[x] = abuf[:, CO * r:CO * (r + 1)]

    pass_x(NEAR[4:])

    lane = lax.broadcasted_iota(jnp.int32, (1, POS), 1)
    hh = lax.rem(lane, H)
    tt = lax.rem(lane // H, T)
    low = lane < COL

    def half_product(h):
        cols = pl.ds(pl.multiple_of(h * HALF, HALF), HALF)
        return jnp.dot(k_ref[:, cols], gall[h].reshape(HALF, POS), preferred_element_type=jnp.float32)

    load_k.wait()
    sib0.wait_recv()
    prod[...] = half_product(zh)
    for c in gy1:
        c.wait_recv()
    sib1 = to_core(1 - zh, 1)
    sib1.wait_recv()
    prod[...] += half_product(1 - zh)

    def tap(a, c, e):
        r = ((a * 3 + c) * 3 + e) * CI
        return prod[r:r + CI, :]

    def tap_sum(e):
        total = None
        for a in range(3):
            part = tap(a, 1, e)
            part += jnp.where(hh != H - 1, shift_lanes(tap(a, 0, e), -1), 0.0)
            part += jnp.where(hh != 0, shift_lanes(tap(a, 2, e), 1), 0.0)
            if a == 0:
                part = jnp.where(tt != T - 1, shift_lanes(part, -H), 0.0)
            elif a == 2:
                part = jnp.where(tt != 0, shift_lanes(part, H), 0.0)
            total = part if total is None else total + part
        return total

    sum0, sum2 = tap_sum(0), tap_sum(2)
    zbuf[...] = jnp.where(low, sum0, sum2)
    to_left = go(remote(zbuf, zr, ha_s.at[0], ha_r.at[0], left_id))
    to_right = go(remote(zbuf, zl, ha_s.at[1], ha_r.at[1], right_id))

    def ay_copy(d):
        slab = gg.at[y]
        return remote(slab, slab, ay_s.at[d], ay_r.at[d], y_ids[d])

    def ac_copy(d):
        slab = gg.at[lax.rem(y + NY - d, NY)]
        return remote(slab, slab, ac_s.at[d], ac_r.at[d], sib_id)

    @pl.when(carries)
    def _():
        @pl.when(jnp.logical_not(b_self))
        def _():
            b_copy(0).wait_recv()
        for d in range(NY - 1):
            ay_copy(d).start()
        ac_copy(0).start()

    mid = tap_sum(1)
    inner = jnp.where(low, sum2, sum0)
    for c in xx:
        c.wait_recv()
    zero = jnp.zeros((), jnp.bfloat16)

    @pl.loop(0, NX * NZ)
    def _(i):
        xb = xg[i // NZ, lax.rem(i, NZ)]
        xs[i, 0:CI] = jnp.where(hh != 0, shift_lanes(xb, 1), zero)
        xs[i, CI:2 * CI] = xb
        xs[i, 2 * CI:] = jnp.where(hh != H - 1, shift_lanes(xb, -1), zero)

    @pl.when(carries)
    def _():
        for d in range(NY - 1):
            ay_copy(d).wait_recv()
            ac_copy(d + 1).start()

    to_left.wait_recv()
    to_right.wait_recv()
    grad = mid + shift_lanes(inner + jnp.where(low, zr[...], zl[...]), COL)
    grad = grad.astype(jnp.bfloat16)
    for w in range(W):
        for t in range(T):
            o = w * COL + t * H
            gin_ref[t, w] = grad[:, o:o + H]

    @pl.when(jnp.logical_not(carries))
    def _():
        for d in range(NY):
            ac_copy(d).wait_recv()

    acc[...] = jnp.zeros_like(acc)

    @pl.loop(0, NZ)
    def _(zz):
        for xn in range(NX):
            here = gg[xn, zz]
            after = gg[xn + 1, zz] if xn < NX - 1 else gg[0, lax.rem(zz + 1, NZ)]
            before = gg[xn - 1, zz] if xn > 0 else gg[NX - 1, lax.rem(zz + NZ - 1, NZ)]
            rh = shift_lanes(here, COL)
            e0 = jnp.where(low, rh, shift_lanes(after, COL))
            e2 = jnp.where(low, shift_lanes(before, COL), rh)
            ge = jnp.concatenate([e0, here, e2], axis=0)
            a0 = jnp.where(tt != T - 1, shift_lanes(ge, -H), zero)
            a2 = jnp.where(tt != 0, shift_lanes(ge, H), zero)
            gs = jnp.concatenate([a0, ge, a2], axis=0)
            acc[...] += lax.dot_general(
                gs, xs[xn * NZ + zz], (((1,), (1,)), ((), ())), preferred_element_type=jnp.float32)

    for a in range(3):
        for e in range(3):
            r = (a * 3 + e) * CO
            for c in range(3):
                gk_ref[(a * 3 + c) * 3 + e] = acc[r:r + CO, c * CI:(c + 1) * CI] * rscale

    for c in sends:
        c.wait_send()

    @pl.when(a_z != z)
    def _():
        a_near().wait_send()

    @pl.when(turn)
    def _():
        for r in range(2):
            @pl.when(jnp.logical_not(b_here(r)))
            def _():
                b_copy(r).wait_send()

    @pl.when(carries)
    def _():
        for d in range(NY - 1):
            ay_copy(d).wait_send()
        for d in range(NY):
            ac_copy(d).wait_send()


def body(inputs, grad_out, weights):
    rscale = 1.0 / math.sqrt(T * H * W * NX * NZ)
    xt = inputs.transpose(0, 1, 3, 4, 2).reshape(T, W, CI, H)
    gt = grad_out.transpose(0, 1, 3, 4, 2).reshape(T, W, CI, H)
    kt = weights.reshape(27 * CI, NH * HALF)
    dma = pltpu.SemaphoreType.DMA
    bf16, f32 = jnp.bfloat16, jnp.float32
    gin, gk = pl.pallas_call(
        functools.partial(kernel, rscale),
        out_shape=(jax.ShapeDtypeStruct((T, W, CI, H), bf16),
                   jax.ShapeDtypeStruct((27, CO, CI), f32)),
        in_specs=[pl.BlockSpec(memory_space=pltpu.MemorySpace.HBM)] * 3,
        out_specs=(pl.BlockSpec(memory_space=pltpu.VMEM),) * 2,
        scratch_shapes=[
            pltpu.VMEM((T, W, CI, H), bf16),
            pltpu.VMEM((T, W, CI, H), bf16),
            pltpu.VMEM((27 * CI, NH * HALF), bf16),
            pltpu.VMEM((NX, NZ, CI, POS), bf16),
            pltpu.VMEM((NX * NZ, 3 * CI, POS), bf16),
            pltpu.VMEM((NH, NY, 2, CI, POS), bf16),
            pltpu.VMEM((NZ, CI, POS), bf16),
            pltpu.VMEM((NX, NZ, CO, POS), bf16),
            pltpu.VMEM((27 * CI, POS), f32),
            pltpu.VMEM((CI, POS), f32),
            pltpu.VMEM((CI, POS), f32),
            pltpu.VMEM((CI, POS), f32),
            pltpu.VMEM((9 * CO, 3 * CI), f32),
            dma((3,)), dma, dma, dma((2, NY - 1)), dma((2, NY - 1)), dma((2,)), dma((2,)),
            dma((NZ - 1,)), dma((NZ - 1,)), dma((NZ, NX - 1)), dma((NZ, NX - 1)),
            dma((2,)), dma((NZ,)), dma((2,)), dma,
            dma((NY - 1,)), dma((NY - 1,)), dma((NY,)), dma((NY,)), dma((2,)), dma((2,)),
        ],
        compiler_params=pltpu.CompilerParams(
            collective_id=0, has_side_effects=True, vmem_limit_bytes=60 << 20),
    )(xt, gt, kt)
    grad_in = gin.reshape(1, T, W, CI, H).transpose(0, 1, 4, 2, 3)
    grad_kernel = gk.reshape(3, 3, 3, CO, CI).transpose(0, 1, 2, 4, 3)
    return grad_in, grad_kernel


def solution(mesh):
    return jax.shard_map(
        body,
        mesh=mesh,
        in_specs=(
            P(None, None, None, "lon", "ch"),
            P(None, None, None, "lon", "ch"),
            P(None, None, None, "ch", None),
        ),
        out_specs=(P(None, None, None, "lon", "ch"), P(None, None, None, "ch", "lon")),
        check_vma=False,
    )
```

```python
import functools
import math

import jax
import jax.numpy as jnp
from jax import lax
from jax.experimental import pallas as pl
from jax.experimental.pallas import tpu as pltpu
from jax.sharding import PartitionSpec as P

NX, NZ, NY, NH = 4, 8, 4, 2
MESH = pl.DeviceIdType.MESH
T, H, W, CI, CO = 4, 48, 2, 32, 16
COL = T * H
POS = W * COL
HALF = NY * 2 * CI
NEAR = (0, 6, 1, 5, 2, 4, 3)


def shift_lanes(v, s):
    n = v.shape[1]
    s = s % n
    if s == 0:
        return v
    return jnp.concatenate([v[:, n - s:], v[:, :n - s]], axis=1)


def pack(ref):
    return jnp.concatenate([ref[t, w] for w in range(W) for t in range(T)], axis=1)


def kernel(rscale, x_hbm, g_hbm, k_hbm, gin_ref, gk_ref,
           x_ref, g_ref, k_ref, xg, xs, gall, abuf, gg, prod, zbuf, zl, zr, acc,
           load_s, swap_s, swap_r, gy_s, gy_r, core_s, core_r,
           xz_s, xz_r, xx_s, xx_r, a_s, a_r, b_s, b_r, ay_s, ay_r, ac_s, ac_r, ha_s, ha_r):
    lon, ch = lax.axis_index("lon"), lax.axis_index("ch")
    z, x = lon // NX, lax.rem(lon, NX)
    zh, y, core = ch // (2 * NY), lax.rem(ch // 2, NY), lax.rem(ch, 2)

    def at(z=z, x=x, zh=zh, y=y, core=core):
        return (z * NX + x, (zh * NY + y) * 2 + core)

    swap_id = at(zh=1 - zh)
    sib_id = at(core=1 - core)
    left_id = (lax.rem(lon + NX * NZ - 1, NX * NZ), ch)
    right_id = (lax.rem(lon + 1, NX * NZ), ch)
    y_ids = [at(y=lax.rem(y + d, NY)) for d in range(1, NY)]
    z_ids = [at(z=lax.rem(z + d, NZ)) for d in range(1, NZ)]
    x_ids = [at(x=lax.rem(x + d, NX)) for d in range(1, NX)]
    partners = [swap_id, sib_id, left_id, right_id] + y_ids + z_ids + x_ids

    turn = y == lax.rem(z, NY)
    home = zh == z // NY
    carries = core == x // 2
    b_from = at(x=y, y=lax.rem(z, NY))
    b_self = turn & (x == y)

    barrier = pltpu.get_barrier_semaphore()

    def greet(dev):
        pl.semaphore_signal(barrier, inc=1, device_id=dev, device_id_type=MESH)

    for dev in partners:
        greet(dev)

    @pl.when(turn & jnp.logical_not(home))
    def _():
        for s in range(NZ):
            greet(at(z=s, zh=1 - zh))

    @pl.when(carries & jnp.logical_not(b_self))
    def _():
        greet(b_from)

    load_g = pltpu.make_async_copy(g_hbm, g_ref, load_s.at[0])
    load_x = pltpu.make_async_copy(x_hbm, x_ref, load_s.at[1])
    load_k = pltpu.make_async_copy(k_hbm, k_ref, load_s.at[2])
    load_g.start()
    load_x.start()
    load_k.start()

    def remote(src, dst, ss, rs, dev):
        return pltpu.make_async_remote_copy(
            src_ref=src, dst_ref=dst, send_sem=ss, recv_sem=rs, device_id=dev, device_id_type=MESH)

    load_g.wait()
    gall[zh, y, core] = pack(g_ref)
    load_x.wait()
    xg[x, z] = pack(x_ref)
    pl.semaphore_wait(barrier, len(partners) + 1 + jnp.where(turn, 2 - (carries & (x == y)).astype(jnp.int32), 0))

    sends = []

    def go(copy):
        copy.start()
        sends.append(copy)
        return copy

    mine = gall.at[zh, y, core]
    swap = go(remote(mine, mine, swap_s, swap_r, swap_id))
    a_z = zh * NY + y
    go(remote(mine, abuf.at[z], a_s.at[0], a_r.at[z], at(z=a_z, zh=1 - zh)))

    def a_near():
        return remote(mine, abuf.at[z], a_s.at[1], a_r.at[z], at(z=a_z))

    @pl.when(a_z != z)
    def _():
        a_near().start()

    @pl.when(a_z == z)
    def _():
        abuf[z] = gall[zh, y, core]

    gy = [go(remote(mine, mine, gy_s.at[0, d], gy_r.at[0, d], y_ids[d])) for d in range(NY - 1)]

    def pass_x(ds):
        for d in ds:
            xz[d].wait_recv()
            blk = xg.at[x, lax.rem(z + NZ - 1 - d, NZ)]
            for e in range(NX - 1):
                xx.append(go(remote(blk, blk, xx_s.at[d + 1, e], xx_r.at[d + 1, e], x_ids[e])))

    def to_core(h, i):
        part = gall.at[h, :, core]
        return go(remote(part, part, core_s.at[i], core_r.at[i], sib_id))

    for c in gy:
        c.wait_recv()
    sib0 = to_core(zh, 0)
    own = xg.at[x, z]
    xz = {d: go(remote(own, own, xz_s.at[d], xz_r.at[d], z_ids[d])) for d in NEAR}
    xx = [go(remote(own, own, xx_s.at[0, e], xx_r.at[0, e], x_ids[e])) for e in range(NX - 1)]
    swap.wait_recv()
    other = gall.at[1 - zh, y, core]
    gy1 = [go(remote(other, other, gy_s.at[1, d], gy_r.at[1, d], y_ids[d])) for d in range(NY - 1)]

    def b_copy(r):
        return remote(abuf.at[:, pl.ds(CO * r, CO)], gg.at[x], b_s.at[r], b_r, at(x=core * 2 + r, y=x))

    def b_here(r):
        return (core * 2 + r == x) & (x == y)

    @pl.when(turn)
    def _():
        for s in range(NZ):
            @pl.when(jnp.logical_not(home & (z == s)))
            def _():
                remote(mine, abuf.at[s], a_s.at[0], a_r.at[s], sib_id).wait_recv()
        for r in range(2):
            @pl.when(jnp.logical_not(b_here(r)))
            def _():
                b_copy(r).start()

            @pl.when(b_here(r))
            def _():
                gg[x] = abuf[:, CO * r:CO * (r + 1)]

    pass_x(NEAR)

    lane = lax.broadcasted_iota(jnp.int32, (1, POS), 1)
    hh = lax.rem(lane, H)
    tt = lax.rem(lane // H, T)
    low = lane < COL

    def half_product(h):
        cols = pl.ds(pl.multiple_of(h * HALF, HALF), HALF)
        return jnp.dot(k_ref[:, cols], gall[h].reshape(HALF, POS), preferred_element_type=jnp.float32)

    load_k.wait()
    sib0.wait_recv()
    prod[...] = half_product(zh)
    def ay_copy(d):
        slab = gg.at[y]
        return remote(slab, slab, ay_s.at[d], ay_r.at[d], y_ids[d])

    def ac_copy(d):
        slab = gg.at[lax.rem(y + NY - d, NY)]
        return remote(slab, slab, ac_s.at[d], ac_r.at[d], sib_id)

    @pl.when(carries)
    def _():
        @pl.when(jnp.logical_not(b_self))
        def _():
            b_copy(0).wait_recv()
        for d in range(NY - 1):
            ay_copy(d).start()
        ac_copy(0).start()

    for c in gy1:
        c.wait_recv()
    sib1 = to_core(1 - zh, 1)
    sib1.wait_recv()
    prod[...] += half_product(1 - zh)

    def tap(a, c, e):
        r = ((a * 3 + c) * 3 + e) * CI
        return prod[r:r + CI, :]

    def tap_sum(e):
        total = None
        for a in range(3):
            part = tap(a, 1, e)
            part += jnp.where(hh != H - 1, shift_lanes(tap(a, 0, e), -1), 0.0)
            part += jnp.where(hh != 0, shift_lanes(tap(a, 2, e), 1), 0.0)
            if a == 0:
                part = jnp.where(tt != T - 1, shift_lanes(part, -H), 0.0)
            elif a == 2:
                part = jnp.where(tt != 0, shift_lanes(part, H), 0.0)
            total = part if total is None else total + part
        return total

    sum0, sum2 = tap_sum(0), tap_sum(2)
    zbuf[...] = jnp.where(low, sum0, sum2)
    to_left = go(remote(zbuf, zr, ha_s.at[0], ha_r.at[0], left_id))
    to_right = go(remote(zbuf, zl, ha_s.at[1], ha_r.at[1], right_id))

    mid = tap_sum(1)
    inner = jnp.where(low, sum2, sum0)
    @pl.when(carries)
    def _():
        for d in range(NY - 1):
            ay_copy(d).wait_recv()
            ac_copy(d + 1).start()

    for c in xx:
        c.wait_recv()
    zero = jnp.zeros((), jnp.bfloat16)

    @pl.loop(0, NX * NZ)
    def _(i):
        xb = xg[i // NZ, lax.rem(i, NZ)]
        xs[i, 0:CI] = jnp.where(hh != 0, shift_lanes(xb, 1), zero)
        xs[i, CI:2 * CI] = xb
        xs[i, 2 * CI:] = jnp.where(hh != H - 1, shift_lanes(xb, -1), zero)

    @pl.when(jnp.logical_not(carries))
    def _():
        for d in range(NY):
            ac_copy(d).wait_recv()

    acc[...] = jnp.zeros_like(acc)

    @pl.loop(0, NZ)
    def _(zz):
        for xn in range(NX):
            here = gg[xn, zz]
            after = gg[xn + 1, zz] if xn < NX - 1 else gg[0, lax.rem(zz + 1, NZ)]
            before = gg[xn - 1, zz] if xn > 0 else gg[NX - 1, lax.rem(zz + NZ - 1, NZ)]
            rh = shift_lanes(here, COL)
            e0 = jnp.where(low, rh, shift_lanes(after, COL))
            e2 = jnp.where(low, shift_lanes(before, COL), rh)
            ge = jnp.concatenate([e0, here, e2], axis=0)
            a0 = jnp.where(tt != T - 1, shift_lanes(ge, -H), zero)
            a2 = jnp.where(tt != 0, shift_lanes(ge, H), zero)
            gs = jnp.concatenate([a0, ge, a2], axis=0)
            acc[...] += lax.dot_general(
                gs, xs[xn * NZ + zz], (((1,), (1,)), ((), ())), preferred_element_type=jnp.float32)

    for a in range(3):
        for e in range(3):
            r = (a * 3 + e) * CO
            for c in range(3):
                gk_ref[(a * 3 + c) * 3 + e] = acc[r:r + CO, c * CI:(c + 1) * CI] * rscale

    to_left.wait_recv()
    to_right.wait_recv()
    grad = mid + shift_lanes(inner + jnp.where(low, zr[...], zl[...]), COL)
    grad = grad.astype(jnp.bfloat16)
    for w in range(W):
        for t in range(T):
            o = w * COL + t * H
            gin_ref[t, w] = grad[:, o:o + H]

    for c in sends:
        c.wait_send()

    @pl.when(a_z != z)
    def _():
        a_near().wait_send()

    @pl.when(turn)
    def _():
        for r in range(2):
            @pl.when(jnp.logical_not(b_here(r)))
            def _():
                b_copy(r).wait_send()

    @pl.when(carries)
    def _():
        for d in range(NY - 1):
            ay_copy(d).wait_send()
        for d in range(NY):
            ac_copy(d).wait_send()


def body(inputs, grad_out, weights):
    rscale = 1.0 / math.sqrt(T * H * W * NX * NZ)
    xt = inputs.transpose(0, 1, 3, 4, 2).reshape(T, W, CI, H)
    gt = grad_out.transpose(0, 1, 3, 4, 2).reshape(T, W, CI, H)
    kt = weights.reshape(27 * CI, NH * HALF)
    dma = pltpu.SemaphoreType.DMA
    bf16, f32 = jnp.bfloat16, jnp.float32
    gin, gk = pl.pallas_call(
        functools.partial(kernel, rscale),
        out_shape=(jax.ShapeDtypeStruct((T, W, CI, H), bf16),
                   jax.ShapeDtypeStruct((27, CO, CI), f32)),
        in_specs=[pl.BlockSpec(memory_space=pltpu.MemorySpace.HBM)] * 3,
        out_specs=(pl.BlockSpec(memory_space=pltpu.VMEM),) * 2,
        scratch_shapes=[
            pltpu.VMEM((T, W, CI, H), bf16),
            pltpu.VMEM((T, W, CI, H), bf16),
            pltpu.VMEM((27 * CI, NH * HALF), bf16),
            pltpu.VMEM((NX, NZ, CI, POS), bf16),
            pltpu.VMEM((NX * NZ, 3 * CI, POS), bf16),
            pltpu.VMEM((NH, NY, 2, CI, POS), bf16),
            pltpu.VMEM((NZ, CI, POS), bf16),
            pltpu.VMEM((NX, NZ, CO, POS), bf16),
            pltpu.VMEM((27 * CI, POS), f32),
            pltpu.VMEM((CI, POS), f32),
            pltpu.VMEM((CI, POS), f32),
            pltpu.VMEM((CI, POS), f32),
            pltpu.VMEM((9 * CO, 3 * CI), f32),
            dma((3,)), dma, dma, dma((2, NY - 1)), dma((2, NY - 1)), dma((2,)), dma((2,)),
            dma((NZ - 1,)), dma((NZ - 1,)), dma((NZ, NX - 1)), dma((NZ, NX - 1)),
            dma((2,)), dma((NZ,)), dma((2,)), dma,
            dma((NY - 1,)), dma((NY - 1,)), dma((NY,)), dma((NY,)), dma((2,)), dma((2,)),
        ],
        compiler_params=pltpu.CompilerParams(
            collective_id=0, has_side_effects=True, vmem_limit_bytes=32 << 20),
    )(*(pltpu.with_memory_space_constraint(v, pltpu.MemorySpace.HBM) for v in (xt, gt, kt)))
    grad_in = gin.reshape(1, T, W, CI, H).transpose(0, 1, 4, 2, 3)
    grad_kernel = gk.reshape(3, 3, 3, CO, CI).transpose(0, 1, 2, 4, 3)
    return grad_in, grad_kernel


def solution(mesh):
    return jax.shard_map(
        body,
        mesh=mesh,
        in_specs=(
            P(None, None, None, "lon", "ch"),
            P(None, None, None, "lon", "ch"),
            P(None, None, None, "ch", None),
        ),
        out_specs=(P(None, None, None, "lon", "ch"), P(None, None, None, "ch", "lon")),
        check_vma=False,
    )
```

```python
import functools
import math

import jax
import jax.numpy as jnp
from jax import lax
from jax.experimental import pallas as pl
from jax.experimental.pallas import tpu as pltpu
from jax.sharding import PartitionSpec as P

NX, NZ, NY, NH = 4, 8, 4, 2
MESH = pl.DeviceIdType.MESH
T, H, W, CI, CO = 4, 48, 2, 32, 16
COL = T * H
POS = W * COL
HALF = NY * 2 * CI
NEAR = (0, 6, 1, 5, 2, 4, 3)


def shift_lanes(v, s):
    n = v.shape[1]
    s = s % n
    if s == 0:
        return v
    return jnp.concatenate([v[:, n - s:], v[:, :n - s]], axis=1)


def pack(ref):
    return jnp.concatenate([ref[t, w] for w in range(W) for t in range(T)], axis=1)


def kernel(rscale, x_hbm, g_hbm, k_hbm, gin_ref, gk_ref,
           x_ref, g_ref, k_ref, xg, xs, gall, abuf, gg, gr, prod, zbuf, zl, zr, acc,
           load_s, swap_s, swap_r, gy_s, gy_r, core_s, core_r,
           xz_s, xz_r, xx_s, xx_r, a_s, a_r, b_s, b_r, ay_s, ay_r, ac_s, ac_r, ha_s, ha_r):
    lon, ch = lax.axis_index("lon"), lax.axis_index("ch")
    z, x = lon // NX, lax.rem(lon, NX)
    zh, y, core = ch // (2 * NY), lax.rem(ch // 2, NY), lax.rem(ch, 2)

    def at(z=z, x=x, zh=zh, y=y, core=core):
        return (z * NX + x, (zh * NY + y) * 2 + core)

    swap_id = at(zh=1 - zh)
    sib_id = at(core=1 - core)
    left_id = (lax.rem(lon + NX * NZ - 1, NX * NZ), ch)
    right_id = (lax.rem(lon + 1, NX * NZ), ch)
    y_ids = [at(y=lax.rem(y + d, NY)) for d in range(1, NY)]
    z_ids = [at(z=lax.rem(z + d, NZ)) for d in range(1, NZ)]
    x_ids = [at(x=lax.rem(x + d, NX)) for d in range(1, NX)]
    partners = [swap_id, sib_id, left_id, right_id] + y_ids + z_ids + x_ids

    turn = y == lax.rem(z, NY)
    home = zh == z // NY
    carries = core == x // 2
    b_from = at(x=y, y=lax.rem(z, NY))
    b_self = turn & (x == y)

    barrier = pltpu.get_barrier_semaphore()

    def greet(dev):
        pl.semaphore_signal(barrier, inc=1, device_id=dev, device_id_type=MESH)

    for dev in partners:
        greet(dev)

    @pl.when(turn & jnp.logical_not(home))
    def _():
        for s in range(NZ):
            greet(at(z=s, zh=1 - zh))

    @pl.when(carries & jnp.logical_not(b_self))
    def _():
        greet(b_from)

    load_g = pltpu.make_async_copy(g_hbm, g_ref, load_s.at[0])
    load_x = pltpu.make_async_copy(x_hbm, x_ref, load_s.at[1])
    load_k = pltpu.make_async_copy(k_hbm, k_ref, load_s.at[2])
    load_g.start()
    load_x.start()
    load_k.start()

    def remote(src, dst, ss, rs, dev):
        return pltpu.make_async_remote_copy(
            src_ref=src, dst_ref=dst, send_sem=ss, recv_sem=rs, device_id=dev, device_id_type=MESH)

    load_g.wait()
    gall[zh, y, core] = pack(g_ref)
    load_x.wait()
    xg[x, z] = pack(x_ref)
    pl.semaphore_wait(barrier, len(partners) + 1 + jnp.where(turn, 2 - (carries & (x == y)).astype(jnp.int32), 0))

    sends = []

    def go(copy):
        copy.start()
        sends.append(copy)
        return copy

    mine = gall.at[zh, y, core]
    swap = go(remote(mine, mine, swap_s, swap_r, swap_id))
    a_z = zh * NY + y
    go(remote(mine, abuf.at[z], a_s.at[0], a_r.at[z], at(z=a_z, zh=1 - zh)))

    def a_near():
        return remote(mine, abuf.at[z], a_s.at[1], a_r.at[z], at(z=a_z))

    @pl.when(a_z != z)
    def _():
        a_near().start()

    @pl.when(a_z == z)
    def _():
        abuf[z] = gall[zh, y, core]

    gy = [go(remote(mine, mine, gy_s.at[0, d], gy_r.at[0, d], y_ids[d])) for d in range(NY - 1)]

    def pass_x(ds):
        for d in ds:
            xz[d].wait_recv()
            blk = xg.at[x, lax.rem(z + NZ - 1 - d, NZ)]
            for e in range(NX - 1):
                xx.append(go(remote(blk, blk, xx_s.at[d + 1, e], xx_r.at[d + 1, e], x_ids[e])))

    def to_core(h, i):
        part = gall.at[h, :, core]
        return go(remote(part, part, core_s.at[i], core_r.at[i], sib_id))

    for c in gy:
        c.wait_recv()
    sib0 = to_core(zh, 0)
    own = xg.at[x, z]
    xz = {d: go(remote(own, own, xz_s.at[d], xz_r.at[d], z_ids[d])) for d in NEAR}
    xx = [go(remote(own, own, xx_s.at[0, e], xx_r.at[0, e], x_ids[e])) for e in range(NX - 1)]
    swap.wait_recv()
    other = gall.at[1 - zh, y, core]
    gy1 = [go(remote(other, other, gy_s.at[1, d], gy_r.at[1, d], y_ids[d])) for d in range(NY - 1)]

    def b_copy(r):
        return remote(abuf.at[:, pl.ds(CO * r, CO)], gg.at[x], b_s.at[r], b_r, at(x=core * 2 + r, y=x))

    def b_here(r):
        return (core * 2 + r == x) & (x == y)

    @pl.when(turn)
    def _():
        for s in range(NZ):
            @pl.when(jnp.logical_not(home & (z == s)))
            def _():
                remote(mine, abuf.at[s], a_s.at[0], a_r.at[s], sib_id).wait_recv()
        for r in range(2):
            @pl.when(jnp.logical_not(b_here(r)))
            def _():
                b_copy(r).start()

            @pl.when(b_here(r))
            def _():
                gg[x] = abuf[:, CO * r:CO * (r + 1)]

    pass_x(NEAR)

    lane = lax.broadcasted_iota(jnp.int32, (1, POS), 1)
    hh = lax.rem(lane, H)
    tt = lax.rem(lane // H, T)
    low = lane < COL
    zero = jnp.zeros((), jnp.bfloat16)

    def shift_x(sl):
        @pl.loop(0, NZ)
        def _(i):
            xb = xg[sl, i]
            xs[sl, i, 0:CI] = jnp.where(hh != 0, shift_lanes(xb, 1), zero)
            xs[sl, i, CI:2 * CI] = xb
            xs[sl, i, 2 * CI:] = jnp.where(hh != H - 1, shift_lanes(xb, -1), zero)


    def half_product(h):
        cols = pl.ds(pl.multiple_of(h * HALF, HALF), HALF)
        return jnp.dot(k_ref[:, cols], gall[h].reshape(HALF, POS), preferred_element_type=jnp.float32)

    load_k.wait()
    sib0.wait_recv()
    prod[...] = half_product(zh)
    def ay_copy(d):
        slab = gg.at[y]
        return remote(slab, slab, ay_s.at[d], ay_r.at[d], y_ids[d])

    def ac_copy(d):
        slab = gg.at[lax.rem(y + NY - d, NY)]
        return remote(slab, slab, ac_s.at[d], ac_r.at[d], sib_id)

    @pl.when(carries)
    def _():
        @pl.when(jnp.logical_not(b_self))
        def _():
            b_copy(0).wait_recv()
        for d in range(NY - 1):
            ay_copy(d).start()
        ac_copy(0).start()

    for c in gy1:
        c.wait_recv()
    sib1 = to_core(1 - zh, 1)
    sib1.wait_recv()
    prod[...] += half_product(1 - zh)

    def tap(a, c, e):
        r = ((a * 3 + c) * 3 + e) * CI
        return prod[r:r + CI, :]

    def tap_sum(e):
        total = None
        for a in range(3):
            part = tap(a, 1, e)
            part += jnp.where(hh != H - 1, shift_lanes(tap(a, 0, e), -1), 0.0)
            part += jnp.where(hh != 0, shift_lanes(tap(a, 2, e), 1), 0.0)
            if a == 0:
                part = jnp.where(tt != T - 1, shift_lanes(part, -H), 0.0)
            elif a == 2:
                part = jnp.where(tt != 0, shift_lanes(part, H), 0.0)
            total = part if total is None else total + part
        return total

    sum0, sum2 = tap_sum(0), tap_sum(2)
    zbuf[...] = jnp.where(low, sum0, sum2)
    to_left = go(remote(zbuf, zr, ha_s.at[0], ha_r.at[0], left_id))
    to_right = go(remote(zbuf, zl, ha_s.at[1], ha_r.at[1], right_id))

    mid = tap_sum(1)
    inner = jnp.where(low, sum2, sum0)

    shift_x(x)

    @pl.when(carries)
    def _():
        for d in range(NY - 1):
            ay_copy(d).wait_recv()
            ac_copy(d + 1).start()

    for d in range(NX - 1):
        for c in xx[d::NX - 1]:
            c.wait_recv()
        shift_x(lax.rem(x + NX - 1 - d, NX))

    @pl.when(jnp.logical_not(carries))
    def _():
        for d in range(NY):
            ac_copy(d).wait_recv()

    acc[...] = jnp.zeros_like(acc)

    @pl.loop(0, NZ)
    def _(zz):
        for xn in range(NX):
            gr[xn, zz] = shift_lanes(gg[xn, zz], COL)

    @pl.loop(0, NZ)
    def _(zz):
        cols = []
        for xn in range(NX):
            here = gr[xn, zz]
            after = gr[xn + 1, zz] if xn < NX - 1 else gr[0, lax.rem(zz + 1, NZ)]
            before = gr[xn - 1, zz] if xn > 0 else gr[NX - 1, lax.rem(zz + NZ - 1, NZ)]
            ge = jnp.concatenate([jnp.where(low, here, after), gg[xn, zz], jnp.where(low, before, here)], axis=0)
            a0 = jnp.where(tt != T - 1, shift_lanes(ge, -H), zero)
            a2 = jnp.where(tt != 0, shift_lanes(ge, H), zero)
            cols.append(jnp.concatenate([a0, ge, a2], axis=0))
        acc[...] += lax.dot_general(
            jnp.concatenate(cols, axis=1), jnp.concatenate([xs[xn, zz] for xn in range(NX)], axis=1),
            (((1,), (1,)), ((), ())), preferred_element_type=jnp.float32)

    for a in range(3):
        for e in range(3):
            r = (a * 3 + e) * CO
            for c in range(3):
                gk_ref[(a * 3 + c) * 3 + e] = acc[r:r + CO, c * CI:(c + 1) * CI] * rscale

    to_left.wait_recv()
    to_right.wait_recv()
    grad = mid + shift_lanes(inner + jnp.where(low, zr[...], zl[...]), COL)
    grad = grad.astype(jnp.bfloat16)
    for w in range(W):
        for t in range(T):
            o = w * COL + t * H
            gin_ref[t, w] = grad[:, o:o + H]

    for c in sends:
        c.wait_send()

    @pl.when(a_z != z)
    def _():
        a_near().wait_send()

    @pl.when(turn)
    def _():
        for r in range(2):
            @pl.when(jnp.logical_not(b_here(r)))
            def _():
                b_copy(r).wait_send()

    @pl.when(carries)
    def _():
        for d in range(NY - 1):
            ay_copy(d).wait_send()
        for d in range(NY):
            ac_copy(d).wait_send()


def body(inputs, grad_out, weights):
    rscale = 1.0 / math.sqrt(T * H * W * NX * NZ)
    xt = inputs.transpose(0, 1, 3, 4, 2).reshape(T, W, CI, H)
    gt = grad_out.transpose(0, 1, 3, 4, 2).reshape(T, W, CI, H)
    kt = weights.reshape(27 * CI, NH * HALF)
    dma = pltpu.SemaphoreType.DMA
    bf16, f32 = jnp.bfloat16, jnp.float32
    gin, gk = pl.pallas_call(
        functools.partial(kernel, rscale),
        out_shape=(jax.ShapeDtypeStruct((T, W, CI, H), bf16),
                   jax.ShapeDtypeStruct((27, CO, CI), f32)),
        in_specs=[pl.BlockSpec(memory_space=pltpu.MemorySpace.HBM)] * 3,
        out_specs=(pl.BlockSpec(memory_space=pltpu.VMEM),) * 2,
        scratch_shapes=[
            pltpu.VMEM((T, W, CI, H), bf16),
            pltpu.VMEM((T, W, CI, H), bf16),
            pltpu.VMEM((27 * CI, NH * HALF), bf16),
            pltpu.VMEM((NX, NZ, CI, POS), bf16),
            pltpu.VMEM((NX, NZ, 3 * CI, POS), bf16),
            pltpu.VMEM((NH, NY, 2, CI, POS), bf16),
            pltpu.VMEM((NZ, CI, POS), bf16),
            pltpu.VMEM((NX, NZ, CO, POS), bf16),
            pltpu.VMEM((NX, NZ, CO, POS), bf16),
            pltpu.VMEM((27 * CI, POS), f32),
            pltpu.VMEM((CI, POS), f32),
            pltpu.VMEM((CI, POS), f32),
            pltpu.VMEM((CI, POS), f32),
            pltpu.VMEM((9 * CO, 3 * CI), f32),
            dma((3,)), dma, dma, dma((2, NY - 1)), dma((2, NY - 1)), dma((2,)), dma((2,)),
            dma((NZ - 1,)), dma((NZ - 1,)), dma((NZ, NX - 1)), dma((NZ, NX - 1)),
            dma((2,)), dma((NZ,)), dma((2,)), dma,
            dma((NY - 1,)), dma((NY - 1,)), dma((NY,)), dma((NY,)), dma((2,)), dma((2,)),
        ],
        compiler_params=pltpu.CompilerParams(
            collective_id=0, has_side_effects=True, vmem_limit_bytes=32 << 20),
    )(*(pltpu.with_memory_space_constraint(v, pltpu.MemorySpace.HBM) for v in (xt, gt, kt)))
    grad_in = gin.reshape(1, T, W, CI, H).transpose(0, 1, 4, 2, 3)
    grad_kernel = gk.reshape(3, 3, 3, CO, CI).transpose(0, 1, 2, 4, 3)
    return grad_in, grad_kernel


def solution(mesh):
    return jax.shard_map(
        body,
        mesh=mesh,
        in_specs=(
            P(None, None, None, "lon", "ch"),
            P(None, None, None, "lon", "ch"),
            P(None, None, None, "ch", None),
        ),
        out_specs=(P(None, None, None, "lon", "ch"), P(None, None, None, "ch", "lon")),
        check_vma=False,
    )
```

```python
import functools
import math

import jax
import jax.numpy as jnp
from jax import lax
from jax.experimental import pallas as pl
from jax.experimental.pallas import tpu as pltpu
from jax.sharding import PartitionSpec as P

NX, NZ, NY, NH = 4, 8, 4, 2
MESH = pl.DeviceIdType.MESH
T, H, W, CI, CO = 4, 48, 2, 32, 16
COL = T * H
POS = W * COL
HALF = NY * 2 * CI
NEAR = (0, 6, 1, 5, 2, 4, 3)


def shift_lanes(v, s):
    n = v.shape[1]
    s = s % n
    if s == 0:
        return v
    return jnp.concatenate([v[:, n - s:], v[:, :n - s]], axis=1)


def pack(ref):
    return jnp.concatenate([ref[t, w] for w in range(W) for t in range(T)], axis=1)


def kernel(rscale, x_hbm, g_hbm, k_hbm, gin_ref, gk_ref,
           x_ref, g_ref, k_ref, xg, xs, gall, abuf, gg, gr, prod, zbuf, zl, zr, acc,
           load_s, swap_s, swap_r, gy_s, gy_r, core_s, core_r,
           xz_s, xz_r, xx_s, xx_r, a_s, a_r, b_s, b_r, ay_s, ay_r, ac_s, ac_r, ha_s, ha_r):
    lon, ch = lax.axis_index("lon"), lax.axis_index("ch")
    z, x = lon // NX, lax.rem(lon, NX)
    zh, y, core = ch // (2 * NY), lax.rem(ch // 2, NY), lax.rem(ch, 2)

    def at(z=z, x=x, zh=zh, y=y, core=core):
        return (z * NX + x, (zh * NY + y) * 2 + core)

    swap_id = at(zh=1 - zh)
    sib_id = at(core=1 - core)
    left_id = (lax.rem(lon + NX * NZ - 1, NX * NZ), ch)
    right_id = (lax.rem(lon + 1, NX * NZ), ch)
    y_ids = [at(y=lax.rem(y + d, NY)) for d in range(1, NY)]
    z_ids = [at(z=lax.rem(z + d, NZ)) for d in range(1, NZ)]
    x_ids = [at(x=lax.rem(x + d, NX)) for d in range(1, NX)]
    partners = [swap_id, sib_id, left_id, right_id] + y_ids + z_ids + x_ids

    turn = y == lax.rem(z, NY)
    home = zh == z // NY
    carries = core == x // 2
    b_from = at(x=y, y=lax.rem(z, NY))
    b_self = turn & (x == y)

    barrier = pltpu.get_barrier_semaphore()

    def greet(dev):
        pl.semaphore_signal(barrier, inc=1, device_id=dev, device_id_type=MESH)

    for dev in partners:
        greet(dev)

    @pl.when(turn & jnp.logical_not(home))
    def _():
        for s in range(NZ):
            greet(at(z=s, zh=1 - zh))

    @pl.when(carries & jnp.logical_not(b_self))
    def _():
        greet(b_from)

    load_g = pltpu.make_async_copy(g_hbm, g_ref, load_s.at[0])
    load_x = pltpu.make_async_copy(x_hbm, x_ref, load_s.at[1])
    load_k = pltpu.make_async_copy(k_hbm, k_ref, load_s.at[2])
    load_g.start()
    load_x.start()
    load_k.start()

    def remote(src, dst, ss, rs, dev):
        return pltpu.make_async_remote_copy(
            src_ref=src, dst_ref=dst, send_sem=ss, recv_sem=rs, device_id=dev, device_id_type=MESH)

    load_g.wait()
    gall[zh, y, core] = pack(g_ref)
    load_x.wait()
    xg[x, z] = pack(x_ref)
    pl.semaphore_wait(barrier, len(partners) + 1 + jnp.where(turn, 2 - (carries & (x == y)).astype(jnp.int32), 0))

    sends = []

    def go(copy):
        copy.start()
        sends.append(copy)
        return copy

    mine = gall.at[zh, y, core]
    a_z = zh * NY + y
    go(remote(mine, abuf.at[z], a_s.at[0], a_r.at[z], at(z=a_z, zh=1 - zh)))

    def a_near():
        return remote(mine, abuf.at[z], a_s.at[1], a_r.at[z], at(z=a_z))

    @pl.when(a_z != z)
    def _():
        a_near().start()

    @pl.when(a_z == z)
    def _():
        abuf[z] = gall[zh, y, core]

    swap = go(remote(mine, mine, swap_s, swap_r, swap_id))
    gy = [go(remote(mine, mine, gy_s.at[0, d], gy_r.at[0, d], y_ids[d])) for d in range(NY - 1)]

    def pass_x(ds):
        for d in ds:
            xz[d].wait_recv()
            blk = xg.at[x, lax.rem(z + NZ - 1 - d, NZ)]
            for e in range(NX - 1):
                xx.append(go(remote(blk, blk, xx_s.at[d + 1, e], xx_r.at[d + 1, e], x_ids[e])))

    def to_core(h, i):
        part = gall.at[h, :, core]
        return go(remote(part, part, core_s.at[i], core_r.at[i], sib_id))

    for c in gy:
        c.wait_recv()
    sib0 = to_core(zh, 0)
    own = xg.at[x, z]
    xz = {d: go(remote(own, own, xz_s.at[d], xz_r.at[d], z_ids[d])) for d in NEAR}
    xx = [go(remote(own, own, xx_s.at[0, e], xx_r.at[0, e], x_ids[e])) for e in range(NX - 1)]
    swap.wait_recv()
    other = gall.at[1 - zh, y, core]
    gy1 = [go(remote(other, other, gy_s.at[1, d], gy_r.at[1, d], y_ids[d])) for d in (1, 0, 2)]

    def b_copy(r):
        return remote(abuf.at[:, pl.ds(CO * r, CO)], gg.at[x], b_s.at[r], b_r, at(x=core * 2 + r, y=x))

    def b_here(r):
        return (core * 2 + r == x) & (x == y)

    @pl.when(turn)
    def _():
        for s in range(NZ):
            @pl.when(jnp.logical_not(home & (z == s)))
            def _():
                remote(mine, abuf.at[s], a_s.at[0], a_r.at[s], sib_id).wait_recv()
        for r in range(2):
            @pl.when(jnp.logical_not(b_here(r)))
            def _():
                b_copy(r).start()

            @pl.when(b_here(r))
            def _():
                gg[x] = abuf[:, CO * r:CO * (r + 1)]

    pass_x(NEAR)

    lane = lax.broadcasted_iota(jnp.int32, (1, POS), 1)
    hh = lax.rem(lane, H)
    tt = lax.rem(lane // H, T)
    low = lane < COL
    zero = jnp.zeros((), jnp.bfloat16)

    def shift_x(sl, i):
        xb = xg[sl, i]
        xs[sl, i, 0:CI] = jnp.where(hh != 0, shift_lanes(xb, 1), zero)
        xs[sl, i, CI:2 * CI] = xb
        xs[sl, i, 2 * CI:] = jnp.where(hh != H - 1, shift_lanes(xb, -1), zero)


    def half_product(h):
        cols = pl.ds(pl.multiple_of(h * HALF, HALF), HALF)
        return jnp.dot(k_ref[:, cols], gall[h].reshape(HALF, POS), preferred_element_type=jnp.float32)

    load_k.wait()
    sib0.wait_recv()
    prod[...] = half_product(zh)
    def ay_copy(d):
        slab = gg.at[y]
        return remote(slab, slab, ay_s.at[d], ay_r.at[d], y_ids[d])

    def ac_copy(d):
        slab = gg.at[lax.rem(y + NY - d, NY)]
        return remote(slab, slab, ac_s.at[d], ac_r.at[d], sib_id)

    @pl.when(carries)
    def _():
        @pl.when(jnp.logical_not(b_self))
        def _():
            b_copy(0).wait_recv()
        for d in (1, 0, 2):
            ay_copy(d).start()
        ac_copy(0).start()

    for c in gy1:
        c.wait_recv()
    sib1 = to_core(1 - zh, 1)
    sib1.wait_recv()
    prod[...] += half_product(1 - zh)

    def tap(a, c, e):
        r = ((a * 3 + c) * 3 + e) * CI
        return prod[r:r + CI, :]

    def tap_sum(e):
        total = None
        for a in range(3):
            part = tap(a, 1, e)
            part += jnp.where(hh != H - 1, shift_lanes(tap(a, 0, e), -1), 0.0)
            part += jnp.where(hh != 0, shift_lanes(tap(a, 2, e), 1), 0.0)
            if a == 0:
                part = jnp.where(tt != T - 1, shift_lanes(part, -H), 0.0)
            elif a == 2:
                part = jnp.where(tt != 0, shift_lanes(part, H), 0.0)
            total = part if total is None else total + part
        return total

    sum0, sum2 = tap_sum(0), tap_sum(2)
    zbuf[...] = jnp.where(low, sum0, sum2)
    to_left = go(remote(zbuf, zr, ha_s.at[0], ha_r.at[0], left_id))
    to_right = go(remote(zbuf, zl, ha_s.at[1], ha_r.at[1], right_id))

    mid = tap_sum(1)
    inner = jnp.where(low, sum2, sum0)

    @pl.loop(0, NZ)
    def _(i):
        shift_x(x, i)

    @pl.when(carries)
    def _():
        for d in range(NY - 1):
            ay_copy(d).wait_recv()
            ac_copy(d + 1).start()

    for k, d in enumerate((NZ - 1,) + NEAR):
        for c in xx[k * (NX - 1):(k + 1) * (NX - 1)]:
            c.wait_recv()

        @pl.loop(1, NX)
        def _(e):
            shift_x(lax.rem(x + NX - e, NX), lax.rem(z + 2 * NZ - 1 - d, NZ))

    @pl.when(jnp.logical_not(carries))
    def _():
        for d in range(NY):
            ac_copy(d).wait_recv()

    acc[...] = jnp.zeros_like(acc)

    @pl.loop(0, NZ)
    def _(zz):
        for xn in range(NX):
            gr[xn, zz] = shift_lanes(gg[xn, zz], COL)

    @pl.loop(0, NZ)
    def _(zz):
        cols = []
        for xn in range(NX):
            here = gr[xn, zz]
            after = gr[xn + 1, zz] if xn < NX - 1 else gr[0, lax.rem(zz + 1, NZ)]
            before = gr[xn - 1, zz] if xn > 0 else gr[NX - 1, lax.rem(zz + NZ - 1, NZ)]
            ge = jnp.concatenate([jnp.where(low, here, after), gg[xn, zz], jnp.where(low, before, here)], axis=0)
            a0 = jnp.where(tt != T - 1, shift_lanes(ge, -H), zero)
            a2 = jnp.where(tt != 0, shift_lanes(ge, H), zero)
            cols.append(jnp.concatenate([a0, ge, a2], axis=0))
        acc[...] += lax.dot_general(
            jnp.concatenate(cols, axis=1), jnp.concatenate([xs[xn, zz] for xn in range(NX)], axis=1),
            (((1,), (1,)), ((), ())), preferred_element_type=jnp.float32)

    for a in range(3):
        for e in range(3):
            r = (a * 3 + e) * CO
            for c in range(3):
                gk_ref[(a * 3 + c) * 3 + e] = acc[r:r + CO, c * CI:(c + 1) * CI] * rscale

    to_left.wait_recv()
    to_right.wait_recv()
    grad = mid + shift_lanes(inner + jnp.where(low, zr[...], zl[...]), COL)
    grad = grad.astype(jnp.bfloat16)
    for w in range(W):
        for t in range(T):
            o = w * COL + t * H
            gin_ref[t, w] = grad[:, o:o + H]

    for c in sends:
        c.wait_send()

    @pl.when(a_z != z)
    def _():
        a_near().wait_send()

    @pl.when(turn)
    def _():
        for r in range(2):
            @pl.when(jnp.logical_not(b_here(r)))
            def _():
                b_copy(r).wait_send()

    @pl.when(carries)
    def _():
        for d in range(NY - 1):
            ay_copy(d).wait_send()
        for d in range(NY):
            ac_copy(d).wait_send()


def body(inputs, grad_out, weights):
    rscale = 1.0 / math.sqrt(T * H * W * NX * NZ)
    xt = inputs.transpose(0, 1, 3, 4, 2).reshape(T, W, CI, H)
    gt = grad_out.transpose(0, 1, 3, 4, 2).reshape(T, W, CI, H)
    kt = weights.reshape(27 * CI, NH * HALF)
    dma = pltpu.SemaphoreType.DMA
    bf16, f32 = jnp.bfloat16, jnp.float32
    gin, gk = pl.pallas_call(
        functools.partial(kernel, rscale),
        out_shape=(jax.ShapeDtypeStruct((T, W, CI, H), bf16),
                   jax.ShapeDtypeStruct((27, CO, CI), f32)),
        in_specs=[pl.BlockSpec(memory_space=pltpu.MemorySpace.HBM)] * 3,
        out_specs=(pl.BlockSpec(memory_space=pltpu.VMEM),) * 2,
        scratch_shapes=[
            pltpu.VMEM((T, W, CI, H), bf16),
            pltpu.VMEM((T, W, CI, H), bf16),
            pltpu.VMEM((27 * CI, NH * HALF), bf16),
            pltpu.VMEM((NX, NZ, CI, POS), bf16),
            pltpu.VMEM((NX, NZ, 3 * CI, POS), bf16),
            pltpu.VMEM((NH, NY, 2, CI, POS), bf16),
            pltpu.VMEM((NZ, CI, POS), bf16),
            pltpu.VMEM((NX, NZ, CO, POS), bf16),
            pltpu.VMEM((NX, NZ, CO, POS), bf16),
            pltpu.VMEM((27 * CI, POS), f32),
            pltpu.VMEM((CI, POS), f32),
            pltpu.VMEM((CI, POS), f32),
            pltpu.VMEM((CI, POS), f32),
            pltpu.VMEM((9 * CO, 3 * CI), f32),
            dma((3,)), dma, dma, dma((2, NY - 1)), dma((2, NY - 1)), dma((2,)), dma((2,)),
            dma((NZ - 1,)), dma((NZ - 1,)), dma((NZ, NX - 1)), dma((NZ, NX - 1)),
            dma((2,)), dma((NZ,)), dma((2,)), dma,
            dma((NY - 1,)), dma((NY - 1,)), dma((NY,)), dma((NY,)), dma((2,)), dma((2,)),
        ],
        compiler_params=pltpu.CompilerParams(
            collective_id=0, has_side_effects=True, vmem_limit_bytes=32 << 20),
    )(*(pltpu.with_memory_space_constraint(v, pltpu.MemorySpace.HBM) for v in (xt, gt, kt)))
    grad_in = gin.reshape(1, T, W, CI, H).transpose(0, 1, 4, 2, 3)
    grad_kernel = gk.reshape(3, 3, 3, CO, CI).transpose(0, 1, 2, 4, 3)
    return grad_in, grad_kernel


def solution(mesh):
    return jax.shard_map(
        body,
        mesh=mesh,
        in_specs=(
            P(None, None, None, "lon", "ch"),
            P(None, None, None, "lon", "ch"),
            P(None, None, None, "ch", None),
        ),
        out_specs=(P(None, None, None, "lon", "ch"), P(None, None, None, "ch", "lon")),
        check_vma=False,
    )
```

```python
import functools
import math

import jax
import jax.numpy as jnp
from jax import lax
from jax.experimental import pallas as pl
from jax.experimental.pallas import tpu as pltpu
from jax.sharding import PartitionSpec as P

NX, NZ, NY, NH = 4, 8, 4, 2
MESH = pl.DeviceIdType.MESH
T, H, W, CI, CO = 4, 48, 2, 32, 16
COL = T * H
POS = W * COL
HALF = NY * 2 * CI
NEAR = (0, 6, 1, 5, 2, 4, 3)


def shift_lanes(v, s):
    n = v.shape[1]
    s = s % n
    if s == 0:
        return v
    return jnp.concatenate([v[:, n - s:], v[:, :n - s]], axis=1)


def pack(ref):
    return jnp.concatenate([ref[t, w] for w in range(W) for t in range(T)], axis=1)


def kernel(rscale, x_hbm, g_hbm, k_hbm, gin_ref, gk_ref,
           x_ref, g_ref, k_ref, xg, xs, gall, abuf, gg, gr, prod, zbuf, zl, zr, acc,
           load_s, swap_s, swap_r, gy_s, gy_r, core_s, core_r,
           xz_s, xz_r, xx_s, xx_r, a_s, a_r, b_s, b_r, ay_s, ay_r, ac_s, ac_r, ha_s, ha_r):
    lon, ch = lax.axis_index("lon"), lax.axis_index("ch")
    z, x = lon // NX, lax.rem(lon, NX)
    zh, y, core = ch // (2 * NY), lax.rem(ch // 2, NY), lax.rem(ch, 2)

    def at(z=z, x=x, zh=zh, y=y, core=core):
        return (z * NX + x, (zh * NY + y) * 2 + core)

    swap_id = at(zh=1 - zh)
    sib_id = at(core=1 - core)
    left_id = (lax.rem(lon + NX * NZ - 1, NX * NZ), ch)
    right_id = (lax.rem(lon + 1, NX * NZ), ch)
    y_ids = [at(y=lax.rem(y + d, NY)) for d in range(1, NY)]
    z_ids = [at(z=lax.rem(z + d, NZ)) for d in range(1, NZ)]
    x_ids = [at(x=lax.rem(x + d, NX)) for d in range(1, NX)]
    partners = [swap_id, sib_id, left_id, right_id] + y_ids + z_ids + x_ids

    turn = y == lax.rem(z, NY)
    home = zh == z // NY
    carries = core == x // 2
    b_from = at(x=y, y=lax.rem(z, NY))
    b_self = turn & (x == y)

    barrier = pltpu.get_barrier_semaphore()

    def greet(dev):
        pl.semaphore_signal(barrier, inc=1, device_id=dev, device_id_type=MESH)

    for dev in partners:
        greet(dev)

    @pl.when(turn & jnp.logical_not(home))
    def _():
        for s in range(NZ):
            greet(at(z=s, zh=1 - zh))

    @pl.when(carries & jnp.logical_not(b_self))
    def _():
        greet(b_from)

    load_g = pltpu.make_async_copy(g_hbm, g_ref, load_s.at[0])
    load_x = pltpu.make_async_copy(x_hbm, x_ref, load_s.at[1])
    load_k = pltpu.make_async_copy(k_hbm, k_ref, load_s.at[2])
    load_g.start()
    load_x.start()
    load_k.start()

    def remote(src, dst, ss, rs, dev):
        return pltpu.make_async_remote_copy(
            src_ref=src, dst_ref=dst, send_sem=ss, recv_sem=rs, device_id=dev, device_id_type=MESH)

    load_g.wait()
    gall[zh, y, core] = pack(g_ref)
    pl.semaphore_wait(barrier, len(partners) + 1 + jnp.where(turn, 2 - (carries & (x == y)).astype(jnp.int32), 0))

    sends = []

    def go(copy):
        copy.start()
        sends.append(copy)
        return copy

    mine = gall.at[zh, y, core]
    a_z = zh * NY + y
    go(remote(mine, abuf.at[z], a_s.at[0], a_r.at[z], at(z=a_z, zh=1 - zh)))

    def a_near():
        return remote(mine, abuf.at[z], a_s.at[1], a_r.at[z], at(z=a_z))

    @pl.when(a_z != z)
    def _():
        a_near().start()

    @pl.when(a_z == z)
    def _():
        abuf[z] = gall[zh, y, core]

    swap = go(remote(mine, mine, swap_s, swap_r, swap_id))
    gy = [go(remote(mine, mine, gy_s.at[0, d], gy_r.at[0, d], y_ids[d])) for d in range(NY - 1)]

    def pass_x(ds):
        for d in ds:
            xz[d].wait_recv()
            blk = xg.at[x, lax.rem(z + NZ - 1 - d, NZ)]
            for e in range(NX - 1):
                xx.append(go(remote(blk, blk, xx_s.at[d + 1, e], xx_r.at[d + 1, e], x_ids[e])))

    def to_core(h, i):
        part = gall.at[h, :, core]
        return go(remote(part, part, core_s.at[i], core_r.at[i], sib_id))

    load_x.wait()
    xg[x, z] = pack(x_ref)
    for c in gy:
        c.wait_recv()
    sib0 = to_core(zh, 0)
    own = xg.at[x, z]
    xz = {d: go(remote(own, own, xz_s.at[d], xz_r.at[d], z_ids[d])) for d in NEAR}
    xx = [go(remote(own, own, xx_s.at[0, e], xx_r.at[0, e], x_ids[e])) for e in range(NX - 1)]
    swap.wait_recv()
    other = gall.at[1 - zh, y, core]
    gy1 = [go(remote(other, other, gy_s.at[1, d], gy_r.at[1, d], y_ids[d])) for d in (1, 0, 2)]

    def b_copy(r):
        return remote(abuf.at[:, pl.ds(CO * r, CO)], gg.at[x], b_s.at[r], b_r, at(x=core * 2 + r, y=x))

    def b_here(r):
        return (core * 2 + r == x) & (x == y)

    @pl.when(turn)
    def _():
        for s in range(NZ):
            @pl.when(jnp.logical_not(home & (z == s)))
            def _():
                remote(mine, abuf.at[s], a_s.at[0], a_r.at[s], sib_id).wait_recv()
        for r in range(2):
            @pl.when(jnp.logical_not(b_here(r)))
            def _():
                b_copy(r).start()

            @pl.when(b_here(r))
            def _():
                gg[x] = abuf[:, CO * r:CO * (r + 1)]

    pass_x(NEAR)

    lane = lax.broadcasted_iota(jnp.int32, (1, POS), 1)
    hh = lax.rem(lane, H)
    tt = lax.rem(lane // H, T)
    low = lane < COL
    zero = jnp.zeros((), jnp.bfloat16)

    def shift_x(sl, i):
        xb = xg[sl, i]
        xs[sl, i, 0:CI] = jnp.where(hh != 0, shift_lanes(xb, 1), zero)
        xs[sl, i, CI:2 * CI] = xb
        xs[sl, i, 2 * CI:] = jnp.where(hh != H - 1, shift_lanes(xb, -1), zero)


    def half_product(h):
        cols = pl.ds(pl.multiple_of(h * HALF, HALF), HALF)
        return jnp.dot(k_ref[:, cols], gall[h].reshape(HALF, POS), preferred_element_type=jnp.float32)

    load_k.wait()
    sib0.wait_recv()
    prod[...] = half_product(zh)
    def ay_copy(d):
        slab = gg.at[y]
        return remote(slab, slab, ay_s.at[d], ay_r.at[d], y_ids[d])

    def ac_copy(d):
        slab = gg.at[lax.rem(y + NY - d, NY)]
        return remote(slab, slab, ac_s.at[d], ac_r.at[d], sib_id)

    @pl.when(carries)
    def _():
        @pl.when(jnp.logical_not(b_self))
        def _():
            b_copy(0).wait_recv()
        for d in (1, 0, 2):
            ay_copy(d).start()
        ac_copy(0).start()

    for c in gy1:
        c.wait_recv()
    sib1 = to_core(1 - zh, 1)
    sib1.wait_recv()
    prod[...] += half_product(1 - zh)

    def tap(a, c, e):
        r = ((a * 3 + c) * 3 + e) * CI
        return prod[r:r + CI, :]

    def tap_sum(e):
        total = None
        for a in range(3):
            part = tap(a, 1, e)
            part += jnp.where(hh != H - 1, shift_lanes(tap(a, 0, e), -1), 0.0)
            part += jnp.where(hh != 0, shift_lanes(tap(a, 2, e), 1), 0.0)
            if a == 0:
                part = jnp.where(tt != T - 1, shift_lanes(part, -H), 0.0)
            elif a == 2:
                part = jnp.where(tt != 0, shift_lanes(part, H), 0.0)
            total = part if total is None else total + part
        return total

    sum0, sum2 = tap_sum(0), tap_sum(2)
    zbuf[...] = jnp.where(low, sum0, sum2)
    to_left = go(remote(zbuf, zr, ha_s.at[0], ha_r.at[0], left_id))
    to_right = go(remote(zbuf, zl, ha_s.at[1], ha_r.at[1], right_id))

    mid = tap_sum(1)
    inner = jnp.where(low, sum2, sum0)

    @pl.loop(0, NZ)
    def _(i):
        shift_x(x, i)

    @pl.when(carries)
    def _():
        for d in range(NY - 1):
            ay_copy(d).wait_recv()
            ac_copy(d + 1).start()

    for k, d in enumerate((NZ - 1,) + NEAR):
        for c in xx[k * (NX - 1):(k + 1) * (NX - 1)]:
            c.wait_recv()

        @pl.loop(1, NX)
        def _(e):
            shift_x(lax.rem(x + NX - e, NX), lax.rem(z + 2 * NZ - 1 - d, NZ))

    @pl.when(jnp.logical_not(carries))
    def _():
        for d in range(NY):
            ac_copy(d).wait_recv()

    acc[...] = jnp.zeros_like(acc)

    @pl.loop(0, NZ)
    def _(zz):
        for xn in range(NX):
            gr[xn, zz] = shift_lanes(gg[xn, zz], COL)

    @pl.loop(0, NZ)
    def _(zz):
        cols = []
        for xn in range(NX):
            here = gr[xn, zz]
            after = gr[xn + 1, zz] if xn < NX - 1 else gr[0, lax.rem(zz + 1, NZ)]
            before = gr[xn - 1, zz] if xn > 0 else gr[NX - 1, lax.rem(zz + NZ - 1, NZ)]
            ge = jnp.concatenate([jnp.where(low, here, after), gg[xn, zz], jnp.where(low, before, here)], axis=0)
            a0 = jnp.where(tt != T - 1, shift_lanes(ge, -H), zero)
            a2 = jnp.where(tt != 0, shift_lanes(ge, H), zero)
            cols.append(jnp.concatenate([a0, ge, a2], axis=0))
        acc[...] += lax.dot_general(
            jnp.concatenate(cols, axis=1), jnp.concatenate([xs[xn, zz] for xn in range(NX)], axis=1),
            (((1,), (1,)), ((), ())), preferred_element_type=jnp.float32)

    for a in range(3):
        for e in range(3):
            r = (a * 3 + e) * CO
            for c in range(3):
                gk_ref[(a * 3 + c) * 3 + e] = acc[r:r + CO, c * CI:(c + 1) * CI] * rscale

    to_left.wait_recv()
    to_right.wait_recv()
    grad = mid + shift_lanes(inner + jnp.where(low, zr[...], zl[...]), COL)
    grad = grad.astype(jnp.bfloat16)
    for w in range(W):
        for t in range(T):
            o = w * COL + t * H
            gin_ref[t, w] = grad[:, o:o + H]

    for c in sends:
        c.wait_send()

    @pl.when(a_z != z)
    def _():
        a_near().wait_send()

    @pl.when(turn)
    def _():
        for r in range(2):
            @pl.when(jnp.logical_not(b_here(r)))
            def _():
                b_copy(r).wait_send()

    @pl.when(carries)
    def _():
        for d in range(NY - 1):
            ay_copy(d).wait_send()
        for d in range(NY):
            ac_copy(d).wait_send()


def body(inputs, grad_out, weights):
    rscale = 1.0 / math.sqrt(T * H * W * NX * NZ)
    xt = inputs.transpose(0, 1, 3, 4, 2).reshape(T, W, CI, H)
    gt = grad_out.transpose(0, 1, 3, 4, 2).reshape(T, W, CI, H)
    kt = weights.reshape(27 * CI, NH * HALF)
    dma = pltpu.SemaphoreType.DMA
    bf16, f32 = jnp.bfloat16, jnp.float32
    gin, gk = pl.pallas_call(
        functools.partial(kernel, rscale),
        out_shape=(jax.ShapeDtypeStruct((T, W, CI, H), bf16),
                   jax.ShapeDtypeStruct((27, CO, CI), f32)),
        in_specs=[pl.BlockSpec(memory_space=pltpu.MemorySpace.HBM)] * 3,
        out_specs=(pl.BlockSpec(memory_space=pltpu.VMEM),) * 2,
        scratch_shapes=[
            pltpu.VMEM((T, W, CI, H), bf16),
            pltpu.VMEM((T, W, CI, H), bf16),
            pltpu.VMEM((27 * CI, NH * HALF), bf16),
            pltpu.VMEM((NX, NZ, CI, POS), bf16),
            pltpu.VMEM((NX, NZ, 3 * CI, POS), bf16),
            pltpu.VMEM((NH, NY, 2, CI, POS), bf16),
            pltpu.VMEM((NZ, CI, POS), bf16),
            pltpu.VMEM((NX, NZ, CO, POS), bf16),
            pltpu.VMEM((NX, NZ, CO, POS), bf16),
            pltpu.VMEM((27 * CI, POS), f32),
            pltpu.VMEM((CI, POS), f32),
            pltpu.VMEM((CI, POS), f32),
            pltpu.VMEM((CI, POS), f32),
            pltpu.VMEM((9 * CO, 3 * CI), f32),
            dma((3,)), dma, dma, dma((2, NY - 1)), dma((2, NY - 1)), dma((2,)), dma((2,)),
            dma((NZ - 1,)), dma((NZ - 1,)), dma((NZ, NX - 1)), dma((NZ, NX - 1)),
            dma((2,)), dma((NZ,)), dma((2,)), dma,
            dma((NY - 1,)), dma((NY - 1,)), dma((NY,)), dma((NY,)), dma((2,)), dma((2,)),
        ],
        compiler_params=pltpu.CompilerParams(
            collective_id=0, has_side_effects=True, vmem_limit_bytes=32 << 20),
    )(*(pltpu.with_memory_space_constraint(v, pltpu.MemorySpace.HBM) for v in (xt, gt, kt)))
    grad_in = gin.reshape(1, T, W, CI, H).transpose(0, 1, 4, 2, 3)
    grad_kernel = gk.reshape(3, 3, 3, CO, CI).transpose(0, 1, 2, 4, 3)
    return grad_in, grad_kernel


def solution(mesh):
    return jax.shard_map(
        body,
        mesh=mesh,
        in_specs=(
            P(None, None, None, "lon", "ch"),
            P(None, None, None, "lon", "ch"),
            P(None, None, None, "ch", None),
        ),
        out_specs=(P(None, None, None, "lon", "ch"), P(None, None, None, "ch", "lon")),
        check_vma=False,
    )
```

```python
import functools
import math

import jax
import jax.numpy as jnp
from jax import lax
from jax.experimental import pallas as pl
from jax.experimental.pallas import tpu as pltpu
from jax.sharding import PartitionSpec as P

NX, NZ, NY, NH = 4, 8, 4, 2
MESH = pl.DeviceIdType.MESH
T, H, W, CI, CO = 4, 48, 2, 32, 16
COL = T * H
POS = W * COL
HALF = NY * 2 * CI
NEAR = (0, 6, 1, 5, 2, 4, 3)


def shift_lanes(v, s):
    n = v.shape[1]
    s = s % n
    if s == 0:
        return v
    return jnp.concatenate([v[:, n - s:], v[:, :n - s]], axis=1)


def pack(ref):
    return jnp.concatenate([ref[t, w] for w in range(W) for t in range(T)], axis=1)


def kernel(rscale, x_hbm, g_hbm, k_hbm, gin_ref, gk_ref,
           x_ref, g_ref, k_ref, xg, xs, gall, abuf, gg, gr, prod, zbuf, zl, zr, acc,
           load_s, swap_s, swap_r, gy_s, gy_r, core_s, core_r,
           xz_s, xz_r, xx_s, xx_r, a_s, a_r, b_s, b_r, ay_s, ay_r, ac_s, ac_r, ha_s, ha_r):
    lon, ch = lax.axis_index("lon"), lax.axis_index("ch")
    z, x = lon // NX, lax.rem(lon, NX)
    zh, y, core = ch // (2 * NY), lax.rem(ch // 2, NY), lax.rem(ch, 2)

    def at(z=z, x=x, zh=zh, y=y, core=core):
        return (z * NX + x, (zh * NY + y) * 2 + core)

    swap_id = at(zh=1 - zh)
    sib_id = at(core=1 - core)
    left_id = (lax.rem(lon + NX * NZ - 1, NX * NZ), ch)
    right_id = (lax.rem(lon + 1, NX * NZ), ch)
    y_ids = [at(y=lax.rem(y + d, NY)) for d in range(1, NY)]
    z_ids = [at(z=lax.rem(z + d, NZ)) for d in range(1, NZ)]
    x_ids = [at(x=lax.rem(x + d, NX)) for d in range(1, NX)]
    partners = [swap_id, sib_id, left_id, right_id] + y_ids + z_ids + x_ids

    turn = y == lax.rem(z, NY)
    home = zh == z // NY
    carries = core == x // 2
    b_from = at(x=y, y=lax.rem(z, NY))
    b_self = turn & (x == y)

    barrier = pltpu.get_barrier_semaphore()

    def greet(dev):
        pl.semaphore_signal(barrier, inc=1, device_id=dev, device_id_type=MESH)

    for dev in partners:
        greet(dev)

    @pl.when(turn & jnp.logical_not(home))
    def _():
        for s in range(NZ):
            greet(at(z=s, zh=1 - zh))

    @pl.when(carries & jnp.logical_not(b_self))
    def _():
        greet(b_from)

    load_g = pltpu.make_async_copy(g_hbm, g_ref, load_s.at[0])
    load_x = pltpu.make_async_copy(x_hbm, x_ref, load_s.at[1])
    load_k = pltpu.make_async_copy(k_hbm, k_ref, load_s.at[2])
    load_g.start()
    load_x.start()
    load_k.start()

    def remote(src, dst, ss, rs, dev):
        return pltpu.make_async_remote_copy(
            src_ref=src, dst_ref=dst, send_sem=ss, recv_sem=rs, device_id=dev, device_id_type=MESH)

    load_g.wait()
    gall[zh, y, core] = pack(g_ref)
    pl.semaphore_wait(barrier, len(partners) + 1 + jnp.where(turn, 2 - (carries & (x == y)).astype(jnp.int32), 0))

    sends = []

    def go(copy):
        copy.start()
        sends.append(copy)
        return copy

    mine = gall.at[zh, y, core]
    a_z = zh * NY + y
    go(remote(mine, abuf.at[z], a_s.at[0], a_r.at[z], at(z=a_z, zh=1 - zh)))

    def a_near():
        return remote(mine, abuf.at[z], a_s.at[1], a_r.at[z], at(z=a_z))

    @pl.when(a_z != z)
    def _():
        a_near().start()

    @pl.when(a_z == z)
    def _():
        abuf[z] = gall[zh, y, core]

    swap = go(remote(mine, mine, swap_s, swap_r, swap_id))
    gy = [go(remote(mine, mine, gy_s.at[0, d], gy_r.at[0, d], y_ids[d])) for d in range(NY - 1)]

    def pass_x(ds):
        for d in ds:
            xz[d].wait_recv()
            blk = xg.at[x, lax.rem(z + NZ - 1 - d, NZ)]
            for e in range(NX - 1):
                xx.append(go(remote(blk, blk, xx_s.at[d + 1, e], xx_r.at[d + 1, e], x_ids[e])))

    def to_core(h, i):
        part = gall.at[h, :, core]
        return go(remote(part, part, core_s.at[i], core_r.at[i], sib_id))

    load_x.wait()
    xg[x, z] = pack(x_ref)
    for c in gy:
        c.wait_recv()
    sib0 = to_core(zh, 0)
    own = xg.at[x, z]
    xz = {d: go(remote(own, own, xz_s.at[d], xz_r.at[d], z_ids[d])) for d in NEAR}
    xx = [go(remote(own, own, xx_s.at[0, e], xx_r.at[0, e], x_ids[e])) for e in range(NX - 1)]
    swap.wait_recv()
    other = gall.at[1 - zh, y, core]
    gy1 = [go(remote(other, other, gy_s.at[1, d], gy_r.at[1, d], y_ids[d])) for d in range(NY - 1)]

    def b_copy(r):
        return remote(abuf.at[:, pl.ds(CO * r, CO)], gg.at[x], b_s.at[r], b_r, at(x=core * 2 + r, y=x))

    def b_here(r):
        return (core * 2 + r == x) & (x == y)

    @pl.when(turn)
    def _():
        for s in range(NZ):
            @pl.when(jnp.logical_not(home & (z == s)))
            def _():
                remote(mine, abuf.at[s], a_s.at[0], a_r.at[s], sib_id).wait_recv()
        for r in range(2):
            @pl.when(jnp.logical_not(b_here(r)))
            def _():
                b_copy(r).start()

            @pl.when(b_here(r))
            def _():
                gg[x] = abuf[:, CO * r:CO * (r + 1)]

    pass_x(NEAR)

    lane = lax.broadcasted_iota(jnp.int32, (1, POS), 1)
    hh = lax.rem(lane, H)
    tt = lax.rem(lane // H, T)
    low = lane < COL
    zero = jnp.zeros((), jnp.bfloat16)

    def shift_x(sl):
        @pl.loop(0, NZ)
        def _(i):
            xb = xg[sl, i]
            xs[sl, i, 0:CI] = jnp.where(hh != 0, shift_lanes(xb, 1), zero)
            xs[sl, i, CI:2 * CI] = xb
            xs[sl, i, 2 * CI:] = jnp.where(hh != H - 1, shift_lanes(xb, -1), zero)


    def half_product(h):
        cols = pl.ds(pl.multiple_of(h * HALF, HALF), HALF)
        return jnp.dot(k_ref[:, cols], gall[h].reshape(HALF, POS), preferred_element_type=jnp.float32)

    load_k.wait()
    sib0.wait_recv()
    prod[...] = half_product(zh)
    def ay_copy(d):
        slab = gg.at[y]
        return remote(slab, slab, ay_s.at[d], ay_r.at[d], y_ids[d])

    def ac_copy(d):
        slab = gg.at[lax.rem(y + NY - d, NY)]
        return remote(slab, slab, ac_s.at[d], ac_r.at[d], sib_id)

    @pl.when(carries)
    def _():
        @pl.when(jnp.logical_not(b_self))
        def _():
            b_copy(0).wait_recv()
        for d in range(NY - 1):
            ay_copy(d).start()
        ac_copy(0).start()

    for c in gy1:
        c.wait_recv()
    sib1 = to_core(1 - zh, 1)
    sib1.wait_recv()
    prod[...] += half_product(1 - zh)

    def tap(a, c, e):
        r = ((a * 3 + c) * 3 + e) * CI
        return prod[r:r + CI, :]

    def tap_sum(e):
        total = None
        for a in range(3):
            part = tap(a, 1, e)
            part += jnp.where(hh != H - 1, shift_lanes(tap(a, 0, e), -1), 0.0)
            part += jnp.where(hh != 0, shift_lanes(tap(a, 2, e), 1), 0.0)
            if a == 0:
                part = jnp.where(tt != T - 1, shift_lanes(part, -H), 0.0)
            elif a == 2:
                part = jnp.where(tt != 0, shift_lanes(part, H), 0.0)
            total = part if total is None else total + part
        return total

    sum0, sum2 = tap_sum(0), tap_sum(2)
    zbuf[...] = jnp.where(low, sum0, sum2)
    to_left = go(remote(zbuf, zr, ha_s.at[0], ha_r.at[0], left_id))
    to_right = go(remote(zbuf, zl, ha_s.at[1], ha_r.at[1], right_id))

    mid = tap_sum(1)
    inner = jnp.where(low, sum2, sum0)

    shift_x(x)

    @pl.when(carries)
    def _():
        for d in range(NY - 1):
            ay_copy(d).wait_recv()
            ac_copy(d + 1).start()

    for d in range(NX - 1):
        for c in xx[d::NX - 1]:
            c.wait_recv()
        shift_x(lax.rem(x + NX - 1 - d, NX))

    @pl.when(jnp.logical_not(carries))
    def _():
        for d in range(NY):
            ac_copy(d).wait_recv()

    acc[...] = jnp.zeros_like(acc)

    @pl.loop(0, NZ)
    def _(zz):
        for xn in range(NX):
            gr[xn, zz] = shift_lanes(gg[xn, zz], COL)

    @pl.loop(0, NZ)
    def _(zz):
        cols = []
        for xn in range(NX):
            here = gr[xn, zz]
            after = gr[xn + 1, zz] if xn < NX - 1 else gr[0, lax.rem(zz + 1, NZ)]
            before = gr[xn - 1, zz] if xn > 0 else gr[NX - 1, lax.rem(zz + NZ - 1, NZ)]
            ge = jnp.concatenate([jnp.where(low, here, after), gg[xn, zz], jnp.where(low, before, here)], axis=0)
            a0 = jnp.where(tt != T - 1, shift_lanes(ge, -H), zero)
            a2 = jnp.where(tt != 0, shift_lanes(ge, H), zero)
            cols.append(jnp.concatenate([a0, ge, a2], axis=0))
        acc[...] += lax.dot_general(
            jnp.concatenate(cols, axis=1), jnp.concatenate([xs[xn, zz] for xn in range(NX)], axis=1),
            (((1,), (1,)), ((), ())), preferred_element_type=jnp.float32)

    for a in range(3):
        for e in range(3):
            r = (a * 3 + e) * CO
            for c in range(3):
                gk_ref[(a * 3 + c) * 3 + e] = acc[r:r + CO, c * CI:(c + 1) * CI] * rscale

    to_left.wait_recv()
    to_right.wait_recv()
    grad = mid + shift_lanes(inner + jnp.where(low, zr[...], zl[...]), COL)
    grad = grad.astype(jnp.bfloat16)
    for w in range(W):
        for t in range(T):
            o = w * COL + t * H
            gin_ref[t, w] = grad[:, o:o + H]

    for c in sends:
        c.wait_send()

    @pl.when(a_z != z)
    def _():
        a_near().wait_send()

    @pl.when(turn)
    def _():
        for r in range(2):
            @pl.when(jnp.logical_not(b_here(r)))
            def _():
                b_copy(r).wait_send()

    @pl.when(carries)
    def _():
        for d in range(NY - 1):
            ay_copy(d).wait_send()
        for d in range(NY):
            ac_copy(d).wait_send()


def body(inputs, grad_out, weights):
    rscale = 1.0 / math.sqrt(T * H * W * NX * NZ)
    xt = inputs.transpose(0, 1, 3, 4, 2).reshape(T, W, CI, H)
    gt = grad_out.transpose(0, 1, 3, 4, 2).reshape(T, W, CI, H)
    kt = weights.reshape(27 * CI, NH * HALF)
    dma = pltpu.SemaphoreType.DMA
    bf16, f32 = jnp.bfloat16, jnp.float32
    gin, gk = pl.pallas_call(
        functools.partial(kernel, rscale),
        out_shape=(jax.ShapeDtypeStruct((T, W, CI, H), bf16),
                   jax.ShapeDtypeStruct((27, CO, CI), f32)),
        in_specs=[pl.BlockSpec(memory_space=pltpu.MemorySpace.HBM)] * 3,
        out_specs=(pl.BlockSpec(memory_space=pltpu.VMEM),) * 2,
        scratch_shapes=[
            pltpu.VMEM((T, W, CI, H), bf16),
            pltpu.VMEM((T, W, CI, H), bf16),
            pltpu.VMEM((27 * CI, NH * HALF), bf16),
            pltpu.VMEM((NX, NZ, CI, POS), bf16),
            pltpu.VMEM((NX, NZ, 3 * CI, POS), bf16),
            pltpu.VMEM((NH, NY, 2, CI, POS), bf16),
            pltpu.VMEM((NZ, CI, POS), bf16),
            pltpu.VMEM((NX, NZ, CO, POS), bf16),
            pltpu.VMEM((NX, NZ, CO, POS), bf16),
            pltpu.VMEM((27 * CI, POS), f32),
            pltpu.VMEM((CI, POS), f32),
            pltpu.VMEM((CI, POS), f32),
            pltpu.VMEM((CI, POS), f32),
            pltpu.VMEM((9 * CO, 3 * CI), f32),
            dma((3,)), dma, dma, dma((2, NY - 1)), dma((2, NY - 1)), dma((2,)), dma((2,)),
            dma((NZ - 1,)), dma((NZ - 1,)), dma((NZ, NX - 1)), dma((NZ, NX - 1)),
            dma((2,)), dma((NZ,)), dma((2,)), dma,
            dma((NY - 1,)), dma((NY - 1,)), dma((NY,)), dma((NY,)), dma((2,)), dma((2,)),
        ],
        compiler_params=pltpu.CompilerParams(
            collective_id=0, has_side_effects=True, vmem_limit_bytes=32 << 20),
    )(*(pltpu.with_memory_space_constraint(v, pltpu.MemorySpace.HBM) for v in (xt, gt, kt)))
    grad_in = gin.reshape(1, T, W, CI, H).transpose(0, 1, 4, 2, 3)
    grad_kernel = gk.reshape(3, 3, 3, CO, CI).transpose(0, 1, 2, 4, 3)
    return grad_in, grad_kernel


def solution(mesh):
    return jax.shard_map(
        body,
        mesh=mesh,
        in_specs=(
            P(None, None, None, "lon", "ch"),
            P(None, None, None, "lon", "ch"),
            P(None, None, None, "ch", None),
        ),
        out_specs=(P(None, None, None, "lon", "ch"), P(None, None, None, "ch", "lon")),
        check_vma=False,
    )
```
